256 devices in a mesh: blk: 32 (over y, x, core), line: 8 (over z).
Axes of the slice: x: 4, y: 4, z: 8, core: 2. Of those that a mesh axis runs over, the one named last changes fastest.
Arguments:
- state: float32 [128, 5, 64, 4096], P('blk', None, 'line'), may hold values from -6 to 6
- viscous: float32 [128, 3, 5], P('blk'), may hold values from 0.1 to 1
- advection: float32 [128, 3, 5], P('blk'), may hold values from -1 to 1
- sweep_inverse: float32 [128, 3, 5, 64, 64], P('blk'), as said below
- face_links: int32 [128, 4, 3], P('blk'), may hold values from -1 to 127, as said below
Outputs:
- update: float32 [128, 5, 64, 4096], P('blk', None, None, 'line')
The draws below stay inside these ranges and needn't reach their ends.
Inputs may be any that keep to these rules, and one draw needn't show every extreme that they name: `face_links`: links are mutual: if face f of block b names (c, g, o) then face g of block c names (b, f, o). A wall face holds -1, 0, 0. No face names a block of its own blk index. For every blk index there is another index whose blocks are named by exactly 2 of its faces, and no pair of indices has more. `sweep_inverse`: per block, direction and field a full 64 x 64 matrix.
All inputs are finite; a program needn't handle non-finite values.
Results may differ from the reference program's by a relative error of at most 0.000071.
Values sent between devices are 32-bit elements; how exact they have to be, the bound alone decides.
A program may use at most 192 MiB of HBM per device.

```python
import math
import jax
import jax.numpy as jnp
from jax import lax

NL = 64
NF = 5
BLK_DEV = 4
CAP = 2
BLOCKS = 128


def draw_sweep_inverse(key, part):
    first_key, second_key = jax.random.split(key)
    shape = (BLOCKS, 3, NF, NL, NL)
    row_index = jnp.arange(NL)[:, None]
    col_index = jnp.arange(NL)[None, :]
    distance = jnp.abs(row_index - col_index).astype(jnp.float32)
    length = NL * 0.5
    roughness = jax.random.uniform(first_key, shape, jnp.float32, 0.5, 1.5)
    diagonal = jax.random.uniform(second_key, shape, jnp.float32, 0.6, 1.4)
    spread = 0.6 / NL * jnp.exp(-distance / length) * roughness
    identity = (row_index == col_index).astype(jnp.float32)
    return identity * diagonal + (1.0 - identity) * spread


def draw_face_links(key, part):
    node_count = BLOCKS // BLK_DEV
    face_count = 4 * BLK_DEV
    group_count = face_count // CAP
    first_key, second_key, third_key, fourth_key = jax.random.split(key, 4)
    half_step = node_count // 2
    shuffled = (jax.random.permutation(first_key, node_count - 1) + 1).astype(jnp.int32)
    half_place = jnp.argmax((shuffled == half_step).astype(jnp.int32)).astype(jnp.int32)
    shuffled = shuffled.at[half_place].set(shuffled[0]).at[0].set(half_step)
    peer_steps = shuffled[:group_count].astype(jnp.int32)
    wall_group = jax.random.randint(second_key, (), 1, group_count).astype(jnp.int32)
    slot_index = jnp.arange(face_count, dtype=jnp.int32)
    xor_step = peer_steps[slot_index // CAP]
    node_index = jnp.arange(node_count, dtype=jnp.int32)[:, None]
    partner = jnp.bitwise_xor(node_index, xor_step[None, :]).astype(jnp.int32)
    lower_node = jnp.minimum(node_index, partner)
    reversal = jax.random.randint(third_key, (node_count, face_count), 0, 2).astype(jnp.int32)[lower_node, slot_index[None, :]]
    node_keys = jax.random.split(fourth_key, node_count)
    slot_face = jax.vmap(lambda one_key: jax.random.permutation(one_key, face_count))(node_keys).astype(jnp.int32)
    theirs = slot_face[partner, slot_index[None, :]]
    neighbor = partner * BLK_DEV + theirs // 4
    values = jnp.stack([neighbor, theirs % 4, reversal], axis=-1).astype(jnp.int32)
    wall_slot = (slot_index // CAP == wall_group)[None, :, None]
    wall_value = jnp.array([-1, 0, 0], dtype=jnp.int32)
    values = jnp.where(wall_slot, wall_value[None, None, :], values).astype(jnp.int32)
    rows_at = (node_index * BLK_DEV + slot_face // 4).astype(jnp.int32)
    faces_at = (slot_face % 4).astype(jnp.int32)
    result = jnp.zeros((BLOCKS, 4, 3), jnp.int32)
    return result.at[rows_at, faces_at].set(values)


def steps_of(key, shape, cuts, low, top_value):
    loudness, own = 1.0, jax.random.fold_in(key, 6)
    for dim, blocks in cuts:
        heights = jnp.exp(jax.random.uniform(jax.random.fold_in(own, dim), (blocks,), jnp.float32, low / len(cuts), top_value / len(cuts)))
        loudness = loudness * jnp.repeat(heights, shape[dim] // blocks).reshape([-1 if axis == dim else 1 for axis in range(len(shape))])
    return loudness


def noise(own_key, shape, deviation, reach, cuts=(), kind=jnp.bfloat16):
    level = steps_of(own_key, shape, cuts, -0.22, 0.18) if cuts else 1.0
    drawn = jax.random.normal(own_key, shape, jnp.float32) * deviation * level
    return jnp.minimum(jnp.maximum(drawn, -reach), reach).astype(kind)


def setup_inputs(seed: int = 0) -> dict:
    streams_of = jax.random.split(jax.random.key(seed), 6)
    return {
        "state": noise(streams_of[0], (BLOCKS, NF, NL, NL * NL), 1.0, 6.0, ((0, 32), (2, 8)), jnp.float32),
        "viscous": jnp.clip(jnp.exp(math.log(1.0) - 2.3025851 * jax.random.uniform(streams_of[1], (BLOCKS, 3, NF), jnp.float32) ** steps_of(streams_of[1], (BLOCKS, 3, NF), ((0, 32),), -0.2, 0.2)), 0.1, 1.0),
        "advection": jnp.clip(jax.random.uniform(streams_of[2], (BLOCKS, 3, NF), jnp.float32, -1.0, 1.0) * steps_of(streams_of[2], (BLOCKS, 3, NF), ((0, 32),), -0.4, 0.0), -1.0, 1.0),
        "sweep_inverse": draw_sweep_inverse(jax.random.fold_in(streams_of[5], 71), 0),
        "face_links": draw_face_links(jax.random.fold_in(streams_of[5], 71), 0),
    }


def block_faces(points):
    return jnp.stack([points[:, :, :, 0, :], points[:, :, :, -1, :], points[:, :, :, :, 0], points[:, :, :, :, -1]], axis=1)


def residual(points, lower_rim, upper_rim, halo_rows, viscous, advection):
    lower_i = jnp.concatenate([lower_rim[:, :, None], points[:, :, :-1]], axis=2)
    upper_i = jnp.concatenate([points[:, :, 1:], upper_rim[:, :, None]], axis=2)
    lower_j = jnp.concatenate([halo_rows[:, 0][:, :, :, None, :], points[:, :, :, :-1]], axis=3)
    upper_j = jnp.concatenate([points[:, :, :, 1:], halo_rows[:, 1][:, :, :, None, :]], axis=3)
    lower_k = jnp.concatenate([halo_rows[:, 2][..., None], points[..., :-1]], axis=4)
    upper_k = jnp.concatenate([points[..., 1:], halo_rows[:, 3][..., None]], axis=4)
    summed = jnp.zeros_like(points)
    sides = ((lower_i, upper_i), (lower_j, upper_j), (lower_k, upper_k))
    for direction in range(3):
        lower_side, upper_side = sides[direction]
        diffuse = viscous[:, direction][:, :, None, None, None]
        carry_speed = advection[:, direction][:, :, None, None, None]
        summed = summed + diffuse * (upper_side - 2.0 * points + lower_side) - carry_speed * 0.5 * (upper_side - lower_side)
    return summed


def sweep_jk(inverse, values):
    after_k = jnp.einsum("bfkl,bfijl->bfijk", inverse[:, 2], values, precision=lax.Precision.HIGHEST, preferred_element_type=jnp.float32)
    return jnp.einsum("bfjl,bfilk->bfijk", inverse[:, 1], after_k, precision=lax.Precision.HIGHEST, preferred_element_type=jnp.float32)


def sweep_i(inverse, values):
    return jnp.einsum("bfil,bfljk->bfijk", inverse[:, 0], values, precision=lax.Precision.HIGHEST, preferred_element_type=jnp.float32)


def reference(state, viscous, advection, sweep_inverse, face_links):
    points = state.reshape(BLOCKS, NF, NL, NL, NL)
    own_faces = block_faces(points)
    neighbor = face_links[..., 0]
    their_face = face_links[..., 1]
    flipped = face_links[..., 2]
    fetched = own_faces[jnp.maximum(neighbor, 0), their_face]
    fetched = jnp.where((flipped == 1)[..., None, None, None], fetched[..., ::-1], fetched)
    halo_rows = jnp.where((neighbor >= 0)[..., None, None, None], fetched, own_faces)

    def one_block(pieces):
        points_one, halo_one, viscous_one, advection_one, inverse_one = pieces
        points_one = points_one[None]
        summed = residual(points_one, points_one[:, :, 0], points_one[:, :, -1], halo_one[None], viscous_one[None], advection_one[None])
        return sweep_i(inverse_one[None], sweep_jk(inverse_one[None], summed))[0]

    update = lax.map(one_block, (points, halo_rows, viscous, advection, sweep_inverse))
    return update.reshape(BLOCKS, NF, NL, NL * NL)
```

```python
import functools

import jax
import jax.numpy as jnp
from jax import lax
from jax.experimental import pallas as pl
from jax.experimental.pallas import tpu as pltpu
from jax.sharding import PartitionSpec as P

MESH = pl.DeviceIdType.MESH
F32 = jnp.float32
BF16 = jnp.bfloat16

NB = 4
NF = 5
NU = NB * NF
NL = 64
ROWS = 8
PAIRS = 32
FACES = 4 * NB
CODES = 128


def link_codes(face_links, blocks_here, count):
    rows = face_links.reshape(FACES, 3)
    neighbor, face, flip = rows[:, 0], rows[:, 1], rows[:, 2]
    linked = neighbor >= 0
    peer = jnp.where(linked, neighbor // blocks_here, -1)
    their = jnp.where(linked, (neighbor % blocks_here) * 4 + face, 0)
    number = jnp.arange(FACES, dtype=jnp.int32)
    same = (peer[:, None] == peer[None, :]) & linked[:, None]
    rank = jnp.sum(same & (number[None, :] < number[:, None]), axis=1)
    place = jnp.sum(same & (their[None, :] < their[:, None]), axis=1)
    target = jnp.arange(2 * count, dtype=jnp.int32)
    hit = (peer[None, :] == target[:, None] // 2) & (rank[None, :] == target[:, None] % 2)
    sent = jnp.sum(jnp.where(hit, 2 * number + flip, 0), axis=1)
    source = jnp.where(linked, peer, 0)
    slot = jnp.where(linked, place, 2)
    tail = jnp.zeros((CODES - 2 * count - 2 * FACES,), jnp.int32)
    return jnp.concatenate([sent, source, slot, tail]).astype(jnp.int32)


def split(value):
    high = value.astype(BF16)
    low = (value - high.astype(F32)).astype(BF16)
    return high, low


def kernel(
    blks, lines,
    codes, viscous, advection, state, inverse, out,
    points, inv, weight_k, weight_j, weight_i, own, table, slots, arrived,
    rim_out, rim_in, halo_j, halo_k, turned, sent, lines_in, result,
    load_sem, inv_sem, rim_send, rim_recv, face_send, face_recv, line_send, line_recv, out_sem,
):
    me = lax.axis_index("blk")
    row = lax.axis_index("line")

    def load(pair):
        return pltpu.make_async_copy(
            state.at[:, :, pl.ds(pair * 128, 128)],
            points.at[:, pl.ds(pair * ROWS, ROWS), :],
            load_sem,
        )

    for pair in range(PAIRS):
        load(pair).start()
    inv_copy = pltpu.make_async_copy(inverse, inv, inv_sem)
    inv_copy.start()

    barrier = pltpu.get_barrier_semaphore()

    def greet_blk(step, carry):
        pl.semaphore_signal(
            barrier, inc=1, device_id=(lax.rem(me + step, blks), row), device_id_type=MESH
        )
        return carry

    def greet_line(step, carry):
        pl.semaphore_signal(
            barrier, inc=1, device_id=(me, lax.rem(row + step, lines)), device_id_type=MESH
        )
        return carry

    lax.fori_loop(1, blks, greet_blk, 0)
    lax.fori_loop(1, lines, greet_line, 0)

    lane = lax.broadcasted_iota(jnp.int32, (ROWS, 128), 1)
    level = lax.broadcasted_iota(jnp.int32, (ROWS, 128), 0)
    left = lane < 64
    even = (lane & 1) == 0

    pltpu.make_async_copy(points, points, load_sem).wait()

    def take_rims(unit, carry):
        rim_out[0, unit] = points[unit, pl.ds(0, PAIRS, stride=ROWS), :]
        rim_out[1, unit] = points[unit, pl.ds(ROWS - 1, PAIRS, stride=ROWS), :]
        return carry

    lax.fori_loop(0, NU, take_rims, 0)

    def merged(values):
        count = 1
        shift = (lane + 1) & 63
        while values.shape[0] > 1:
            pairs = values.reshape(values.shape[0] // 2, 2, ROWS, 128)
            moved = pltpu.roll(pairs[:, 1], 2 * count, axis=2)
            values = jnp.where((shift < 2 * count)[None], pairs[:, 0], moved)
            count *= 2
        return values[0]

    def take_faces(unit, carry):
        block, field = unit // NF, lax.rem(unit, NF)
        cells = points[unit].reshape(PAIRS, ROWS, 128)
        own[2 * block, field] = jnp.where(left, cells[0], cells[PAIRS - 1])
        mixed = merged(cells)
        low = jnp.where(even, mixed, pltpu.roll(mixed, 65, axis=1))
        high = jnp.where(even, pltpu.roll(mixed, 1, axis=1), pltpu.roll(mixed, 66, axis=1))
        own[2 * block + 1, field] = jnp.where(left, low, high)
        return carry

    lax.fori_loop(0, NU, take_faces, 0)

    def fill_table(item, carry):
        pair, field = item // NF, lax.rem(item, NF)
        forward = own[pair, field]
        backward = forward
        for bit in (1, 2, 4, 8, 16, 32):
            backward = jnp.where(
                (lane & bit) != 0,
                pltpu.roll(backward, bit, axis=1),
                pltpu.roll(backward, 128 - bit, axis=1),
            )
        for flip, value in ((0, forward), (1, backward)):
            other = pltpu.roll(value, 64, axis=1)
            table[4 * pair + flip, field] = jnp.where(left, value, other)
            table[4 * pair + 2 + flip, field] = jnp.where(left, other, value)
        return carry

    lax.fori_loop(0, 2 * NB * NF, fill_table, 0)

    pl.semaphore_wait(barrier, blks + lines - 2)

    rims = [
        pltpu.make_async_remote_copy(
            src_ref=rim_out.at[side],
            dst_ref=rim_in.at[1 - side],
            send_sem=rim_send.at[side],
            recv_sem=rim_recv.at[1 - side],
            device_id=(me, lax.rem(row + (lines - 1 if side == 0 else 1), lines)),
            device_id_type=MESH,
        )
        for side in (0, 1)
    ]
    for rim in rims:
        rim.start()

    def send_faces(step, carry):
        target = lax.rem(me + step, blks)
        slots[target] = jnp.where(
            left[None], table[codes[2 * target]], table[codes[2 * target + 1]]
        )
        pltpu.make_async_remote_copy(
            src_ref=slots.at[target],
            dst_ref=arrived.at[me],
            send_sem=face_send,
            recv_sem=face_recv,
            device_id=(target, row),
            device_id_type=MESH,
        ).start()
        return carry

    lax.fori_loop(1, blks, send_faces, 0)

    inv_copy.wait()
    deep = lax.broadcasted_iota(jnp.int32, (NL, 128), 0)
    wide = lax.broadcasted_iota(jnp.int32, (NL, 128), 1)
    ones = jnp.ones((NL, 128), F32)
    zeros = jnp.zeros((NL, 128), F32)
    at_left = jnp.where(deep == wide, ones, zeros).astype(BF16)
    at_right = jnp.where(deep + NL == wide, ones, zeros).astype(BF16)
    column = wide & 63
    order = 2 * (column & 31) + (column >> 5)
    picked = jnp.where(deep == order, ones, zeros)
    pick_left = jnp.where(wide < 64, picked, zeros).astype(BF16)
    pick_right = jnp.where(wide < 64, zeros, picked).astype(BF16)

    def place(value, where):
        return jnp.dot(value, where, preferred_element_type=F32)

    def make_weights(unit, carry):
        block, field = unit // NF, lax.rem(unit, NF)
        base = block * 3 * NF + field
        high, low = split(inv[base + 2 * NF])
        weight_k[unit, 0:64] = place(high, at_left).astype(BF16)
        weight_k[unit, 64:128] = place(high, at_right).astype(BF16)
        weight_k[unit, 128:192] = place(low, at_left).astype(BF16)
        weight_k[unit, 192:256] = place(low, at_right).astype(BF16)
        along_j = jnp.concatenate(
            [
                inv[base + NF, pl.ds(0, PAIRS, stride=2), :],
                inv[base + NF, pl.ds(1, PAIRS, stride=2), :],
            ],
            axis=0,
        )
        high, low = split(along_j)
        weight_j[unit] = (place(high, pick_left) + place(low, pick_right)).astype(BF16)
        high, low = split(inv[base])
        weight_i[unit] = (place(high, at_left) + place(low, at_right)).astype(BF16)
        return carry

    lax.fori_loop(0, NU, make_weights, 0)

    for rim in rims:
        rim.wait()
    pltpu.make_async_copy(
        slots.at[pl.ds(0, blks - 1)], slots.at[pl.ds(0, blks - 1)], face_send
    ).wait()
    pltpu.make_async_copy(
        arrived.at[pl.ds(0, blks - 1)], arrived.at[pl.ds(0, blks - 1)], face_recv
    ).wait()

    whole = (NF, ROWS, 128)

    def facing(face, half):
        source, slot = codes[2 * blks + face], codes[2 * blks + FACES + face]
        value = arrived[source]
        slots_of = jnp.full(whole, slot, jnp.int32)
        value = jnp.where(slots_of == half, value, pltpu.roll(value, 64, axis=2))
        return jnp.where(slots_of == 2, own[face // 2], value)

    for pair in range(2 * NB):
        value = jnp.where(left[None], facing(2 * pair, 0), facing(2 * pair + 1, 1))
        block = pair // 2
        if pair % 2 == 0:
            halo_j[pl.ds(block * NF, NF)] = value
        else:
            far = jnp.where(left[None], value, pltpu.roll(value, 63, axis=2))
            ahead = ((lane >= 63) & (lane < 126))[None]
            near = jnp.where(ahead, pltpu.roll(value, 127, axis=2), pltpu.roll(value, 62, axis=2))
            halo_k[pl.ds(block * NF, NF)] = jnp.where(even[None], far, near)

    first = jnp.full((ROWS, 128), row, jnp.int32) == 0
    last = jnp.full((ROWS, 128), row, jnp.int32) == lines - 1
    top, bottom = level == 0, level == ROWS - 1
    k_low, k_high = (lane & 63) == 0, (lane & 63) == 63
    left_wide = lax.broadcasted_iota(jnp.int32, (PAIRS, 128), 1) < 64

    def line_copy(unit, step):
        target = lax.rem(row + step, lines)
        return pltpu.make_async_remote_copy(
            src_ref=sent.at[unit, pl.ds(target * PAIRS, PAIRS), :],
            dst_ref=lines_in.at[unit, row],
            send_sem=line_send.at[unit],
            recv_sem=line_recv.at[unit],
            device_id=(me, target),
            device_id_type=MESH,
        )

    def sweep_jk(unit, carry):
        block, field = unit // NF, lax.rem(unit, NF)
        ahead, behind = [], []
        middle = jnp.float32(0.0)
        for direction in range(3):
            diffuse = viscous[block, direction, field]
            half_speed = 0.5 * advection[block, direction, field]
            ahead.append(diffuse - half_speed)
            behind.append(diffuse + half_speed)
            middle = middle - 2.0 * diffuse
        j_rows, k_rows = halo_j[unit], halo_k[unit]
        cells = [points[unit, pl.ds(pair * ROWS, ROWS), :] for pair in range(PAIRS)]
        turns = [pltpu.roll(cell, 64, axis=1) for cell in cells]
        summed = []
        for pair in range(PAIRS):
            cell, turn = cells[pair], turns[pair]
            below = jnp.broadcast_to(rim_in[0, unit, pl.ds(pair, 1), :], (ROWS, 128))
            above = jnp.broadcast_to(rim_in[1, unit, pl.ds(pair, 1), :], (ROWS, 128))
            below = jnp.where(first, cell, below)
            above = jnp.where(last, cell, above)
            i_minus = jnp.where(top, below, pltpu.roll(cell, 1, axis=0))
            i_plus = jnp.where(bottom, above, pltpu.roll(cell, ROWS - 1, axis=0))
            j_minus = jnp.where(left, turns[pair - 1] if pair else j_rows, turn)
            j_plus = jnp.where(left, turn, turns[pair + 1] if pair < PAIRS - 1 else j_rows)
            edge = pltpu.roll(k_rows, (128 - 2 * pair) % 128, axis=1) if pair else k_rows
            k_minus = jnp.where(k_low, edge, pltpu.roll(cell, 1, axis=1))
            k_plus = jnp.where(k_high, edge, pltpu.roll(cell, 127, axis=1))
            summed.append(
                middle * cell
                + (ahead[0] * i_plus + behind[0] * i_minus)
                + (ahead[1] * j_plus + behind[1] * j_minus)
                + (ahead[2] * k_plus + behind[2] * k_minus)
            )
        high, low = split(jnp.concatenate(summed, axis=0))
        inverse_k = weight_k[unit]
        both = lax.dot_general(
            jnp.concatenate([high, low], axis=1),
            jnp.concatenate([inverse_k, inverse_k], axis=1),
            (((1,), (1,)), ((), ())),
            preferred_element_type=F32,
        )
        turned[...] = both[:, :128] + both[:, 128:]
        columns = []
        for step in range(0, ROWS, 2):
            one = turned[pl.ds(step, PAIRS, stride=ROWS), :]
            two = turned[pl.ds(step + 1, PAIRS, stride=ROWS), :]
            evens = jnp.where(left_wide, one, pltpu.roll(two, 64, axis=1))
            odds = jnp.where(left_wide, pltpu.roll(one, 64, axis=1), two)
            columns.append(jnp.concatenate([evens, odds], axis=0))
        after = sweep(weight_j[unit], jnp.concatenate(columns, axis=1))
        for step in range(0, ROWS, 2):
            evens = after[:PAIRS, step * 64 : step * 64 + 128]
            odds = after[PAIRS:, step * 64 : step * 64 + 128]
            sent[unit, pl.ds(step, PAIRS, stride=ROWS), :] = jnp.where(
                left_wide, evens, pltpu.roll(odds, 64, axis=1)
            )
            sent[unit, pl.ds(step + 1, PAIRS, stride=ROWS), :] = jnp.where(
                left_wide, pltpu.roll(evens, 64, axis=1), odds
            )
        lines_in[unit, row] = sent[unit, pl.ds(row * PAIRS, PAIRS), :]
        for step in (4, 3, 5, 2, 6, 1, 7):
            line_copy(unit, step).start()
        return carry

    def sweep(weight, value):
        high, low = split(value)
        return jnp.dot(
            jnp.concatenate([weight, weight], axis=1),
            jnp.concatenate([high, high, low, low], axis=0),
            preferred_element_type=F32,
        )

    lax.fori_loop(0, NU, sweep_jk, 0)

    others = pl.ds(0, lines - 1)

    def sweep_i(unit, carry):
        pltpu.make_async_copy(
            lines_in.at[unit, others], lines_in.at[unit, others], line_recv.at[unit]
        ).wait()
        values = lines_in[unit]
        columns = [
            values[:, pair * ROWS : (pair + 1) * ROWS, :].reshape(NL, 128) for pair in range(4)
        ]
        result[unit] = sweep(weight_i[unit], jnp.concatenate(columns, axis=1))
        pltpu.make_async_copy(result.at[unit], out.at[unit], out_sem).start()
        return carry

    lax.fori_loop(0, NU, sweep_i, 0)

    def finish(unit, carry):
        pltpu.make_async_copy(
            lines_in.at[unit, others], lines_in.at[unit, others], line_send.at[unit]
        ).wait()
        return carry

    lax.fori_loop(0, NU, finish, 0)
    pltpu.make_async_copy(result, out, out_sem).wait()


def on_device(state, viscous, advection, sweep_inverse, face_links):
    blks, lines = lax.axis_size("blk"), lax.axis_size("line")
    blocks_here, fields, rows_here, plane = state.shape
    codes = link_codes(face_links, blocks_here, blks)
    smem = pl.BlockSpec(memory_space=pltpu.SMEM)
    anywhere = pl.BlockSpec(memory_space=pl.ANY)
    dma = pltpu.SemaphoreType.DMA
    out = pl.pallas_call(
        functools.partial(kernel, blks, lines),
        out_shape=jax.ShapeDtypeStruct((NU, NL, plane // lines), F32),
        in_specs=[smem, smem, smem, anywhere, anywhere],
        out_specs=anywhere,
        scratch_shapes=[
            pltpu.VMEM((NU, PAIRS * ROWS, 128), F32),
            pltpu.VMEM((3 * NU, NL, NL), F32),
            pltpu.VMEM((NU, 256, 128), BF16),
            pltpu.VMEM((NU, NL, 128), BF16),
            pltpu.VMEM((NU, NL, 128), BF16),
            pltpu.VMEM((2 * NB, NF, ROWS, 128), F32),
            pltpu.VMEM((2 * FACES, NF, ROWS, 128), F32),
            pltpu.VMEM((blks, NF, ROWS, 128), F32),
            pltpu.VMEM((blks, NF, ROWS, 128), F32),
            pltpu.VMEM((2, NU, PAIRS, 128), F32),
            pltpu.VMEM((2, NU, PAIRS, 128), F32),
            pltpu.VMEM((NU, ROWS, 128), F32),
            pltpu.VMEM((NU, ROWS, 128), F32),
            pltpu.VMEM((PAIRS * ROWS, 128), F32),
            pltpu.VMEM((NU, PAIRS * ROWS, 128), F32),
            pltpu.VMEM((NU, lines, PAIRS, 128), F32),
            pltpu.VMEM((NU, NL, plane // lines), F32),
            dma, dma, dma((2,)), dma((2,)), dma, dma, dma((NU,)), dma((NU,)), dma,
        ],
        compiler_params=pltpu.CompilerParams(
            collective_id=0, has_side_effects=True, vmem_limit_bytes=40 * 1024 * 1024
        ),
        name="implicit_update",
    )(
        codes,
        viscous,
        advection,
        state.reshape(NU, rows_here, plane),
        sweep_inverse.reshape(3 * NU, NL, NL),
    )
    return out.reshape(blocks_here, fields, NL, plane // lines)


def solution(mesh):
    in_specs = (
        P("blk", None, "line", None),
        P("blk", None, None),
        P("blk", None, None),
        P("blk", None, None, None, None),
        P("blk", None, None),
    )
    out_specs = P("blk", None, None, "line")
    return jax.shard_map(
        on_device, mesh=mesh, in_specs=in_specs, out_specs=out_specs, check_vma=False
    )
```

```python
import functools

import jax
import jax.numpy as jnp
from jax import lax
from jax.experimental import pallas as pl
from jax.experimental.pallas import tpu as pltpu
from jax.sharding import PartitionSpec as P

MESH = pl.DeviceIdType.MESH
F32 = jnp.float32
BF16 = jnp.bfloat16

NB = 4
NF = 5
NU = NB * NF
NL = 64
ROWS = 8
PAIRS = 32
FACES = 4 * NB
CODES = 128


def link_codes(links, blocks_here, blks):
    lane = lax.broadcasted_iota(jnp.int32, (8, CODES), 1)
    target, slot = lane >> 1, lane & 1
    number = lane & (FACES - 1)
    faces = []
    for face in range(FACES):
        neighbor, their, flip = (links[part, face // 4, face % 4] for part in range(3))
        peer = jnp.where(neighbor >= 0, neighbor // blocks_here, -1)
        faces.append((peer, lax.rem(neighbor, blocks_here) * 4 + their, flip))
    sent = jnp.zeros_like(lane)
    seen = jnp.zeros_like(lane)
    peers = jnp.zeros_like(lane)
    theirs = jnp.zeros_like(lane)
    for face, (peer, their, flip) in enumerate(faces):
        match = target == peer
        sent = jnp.where(match & (seen == slot), 2 * face + flip, sent)
        seen = jnp.where(match, seen + 1, seen)
        peers = jnp.where(number == face, peer, peers)
        theirs = jnp.where(number == face, their, theirs)
    place = jnp.zeros_like(lane)
    for peer, their, _ in faces:
        place = jnp.where((peers == peer) & (theirs > their), place + 1, place)
    source = jnp.where(peers < 0, 0, peers)
    place = jnp.where(peers < 0, 2, place)
    return jnp.where(lane < 2 * blks, sent, jnp.where(lane < 2 * blks + FACES, source, place))


def permuted(value, order):
    return jnp.take_along_axis(value, order, axis=1, mode="promise_in_bounds")


def split(value):
    high = value.astype(BF16)
    low = (value - high.astype(F32)).astype(BF16)
    return high, low


def kernel(
    blks, lines,
    links, viscous, advection, state, inverse, out,
    points, inv, weight_k, weight_j, weight_i, codes_out, codes, table, slots, arrived,
    rim_out, rim_in, halo_j, halo_k, turned, sent, lines_in, result,
    load_sem, inv_sem, codes_sem, rim_send, rim_recv, face_send, face_recv, line_send, line_recv, out_sem,
):
    me = lax.axis_index("blk")
    row = lax.axis_index("line")

    def load(pair):
        return pltpu.make_async_copy(
            state.at[:, :, pl.ds(pair * 128, 128)],
            points.at[:, pl.ds(pair * ROWS, ROWS), :],
            load_sem,
        )

    for pair in range(PAIRS):
        load(pair).start()
    inv_copy = pltpu.make_async_copy(inverse, inv, inv_sem)
    inv_copy.start()

    barrier = pltpu.get_barrier_semaphore()

    def greet_blk(step, carry):
        pl.semaphore_signal(
            barrier, inc=1, device_id=(lax.rem(me + step, blks), row), device_id_type=MESH
        )
        return carry

    def greet_line(step, carry):
        pl.semaphore_signal(
            barrier, inc=1, device_id=(me, lax.rem(row + step, lines)), device_id_type=MESH
        )
        return carry

    lax.fori_loop(1, blks, greet_blk, 0)
    lax.fori_loop(1, lines, greet_line, 0)

    codes_out[...] = link_codes(links, NB, blks)
    codes_copy = pltpu.make_async_copy(codes_out, codes, codes_sem)
    codes_copy.start()

    lane = lax.broadcasted_iota(jnp.int32, (ROWS, 128), 1)
    level = lax.broadcasted_iota(jnp.int32, (ROWS, 128), 0)
    left = lane < 64
    even = (lane & 1) == 0
    point = lane & 63

    pltpu.make_async_copy(points, points, load_sem).wait()

    def take_rims(block, carry):
        for field in range(NF):
            unit = block * NF + field
            rim_out[0, unit] = points[unit, pl.ds(0, PAIRS, stride=ROWS), :]
            rim_out[1, unit] = points[unit, pl.ds(ROWS - 1, PAIRS, stride=ROWS), :]
        return carry

    lax.fori_loop(0, NB, take_rims, 0)

    key = ((lane + 1) & 63) >> 1
    bits = [((key >> bit) & 1) == 1 for bit in range(5)]

    def mixed_low(where):
        return (where & 1) * 64 + (where & 62)

    low_order = [mixed_low(point), mixed_low(63 - point)]
    k_orders = low_order + [(order + 63) & 127 for order in low_order]
    j_orders = [point, 63 - point, 64 + point, 127 - point]

    def take_faces(block, carry):
        for field in range(NF):
            unit = block * NF + field
            cells = [points[unit, pl.ds(pair * ROWS, ROWS), :] for pair in range(PAIRS)]
            j_faces = jnp.where(left, cells[0], cells[PAIRS - 1])
            tiles = [pltpu.roll(cell, 2 * pair, axis=1) for pair, cell in enumerate(cells)]
            for bit in bits:
                tiles = [
                    jnp.where(bit, high, low) for low, high in zip(tiles[::2], tiles[1::2])
                ]
            for number, order in enumerate(j_orders):
                table[8 * block + number, field] = permuted(j_faces, order)
            for number, order in enumerate(k_orders):
                table[8 * block + 4 + number, field] = permuted(tiles[0], order)
        return carry

    lax.fori_loop(0, NB, take_faces, 0)
    codes_copy.wait()

    def fill_slots(target, carry):
        slots[target] = jnp.where(
            left[None], table[codes[0, 2 * target]], table[codes[0, 2 * target + 1]]
        )
        return carry

    lax.fori_loop(0, blks, fill_slots, 0)

    pl.semaphore_wait(barrier, blks + lines - 2)

    def rim_copy(block, side):
        rows = pl.ds(block * NF, NF)
        return pltpu.make_async_remote_copy(
            src_ref=rim_out.at[side, rows],
            dst_ref=rim_in.at[1 - side, rows],
            send_sem=rim_send.at[side, block],
            recv_sem=rim_recv.at[1 - side, block],
            device_id=(me, lax.rem(row + (lines - 1 if side == 0 else 1), lines)),
            device_id_type=MESH,
        )

    for block in range(NB):
        for side in (0, 1):
            rim_copy(block, side).start()

    def send_faces(step, carry):
        target = lax.rem(me + step, blks)
        pltpu.make_async_remote_copy(
            src_ref=slots.at[target],
            dst_ref=arrived.at[me],
            send_sem=face_send,
            recv_sem=face_recv,
            device_id=(target, row),
            device_id_type=MESH,
        ).start()
        return carry

    lax.fori_loop(1, blks, send_faces, 0)

    inv_copy.wait()
    deep = lax.broadcasted_iota(jnp.int32, (NL, 128), 0)
    wide = lax.broadcasted_iota(jnp.int32, (NL, 128), 1)
    ones = jnp.ones((NL, 128), F32)
    zeros = jnp.zeros((NL, 128), F32)
    at_left = jnp.where(deep == wide, ones, zeros).astype(BF16)
    at_right = jnp.where(deep + NL == wide, ones, zeros).astype(BF16)
    column = wide & 63
    order = 2 * (column & 31) + (column >> 5)
    picked = jnp.where(deep == order, ones, zeros)
    pick_left = jnp.where(wide < 64, picked, zeros).astype(BF16)
    pick_right = jnp.where(wide < 64, zeros, picked).astype(BF16)

    def place(value, where):
        return jnp.dot(value, where, preferred_element_type=F32)

    def make_weights(unit, carry):
        block, field = unit // NF, lax.rem(unit, NF)
        base = block * 3 * NF + field
        high, low = split(inv[base + 2 * NF])
        weight_k[unit, 0:64] = place(high, at_left).astype(BF16)
        weight_k[unit, 64:128] = place(high, at_right).astype(BF16)
        weight_k[unit, 128:192] = place(low, at_left).astype(BF16)
        weight_k[unit, 192:256] = place(low, at_right).astype(BF16)
        along_j = jnp.concatenate(
            [
                inv[base + NF, pl.ds(0, PAIRS, stride=2), :],
                inv[base + NF, pl.ds(1, PAIRS, stride=2), :],
            ],
            axis=0,
        )
        high, low = split(along_j)
        weight_j[unit] = (place(high, pick_left) + place(low, pick_right)).astype(BF16)
        high, low = split(inv[base])
        weight_i[unit] = (place(high, at_left) + place(low, at_right)).astype(BF16)
        return carry

    lax.fori_loop(0, NU, make_weights, 0)

    pltpu.make_async_copy(
        slots.at[pl.ds(0, blks - 1)], slots.at[pl.ds(0, blks - 1)], face_send
    ).wait()
    pltpu.make_async_copy(
        arrived.at[pl.ds(0, blks - 1)], arrived.at[pl.ds(0, blks - 1)], face_recv
    ).wait()

    whole = (NF, ROWS, 128)

    def facing(face, half):
        source = codes[0, 2 * blks + face]
        slots_of = jnp.full(whole, codes[0, 2 * blks + FACES + face], jnp.int32)
        value = arrived[source]
        value = jnp.where(slots_of == half, value, pltpu.roll(value, 64, axis=2))
        return jnp.where(slots_of == 2, table[2 * face], value)

    mixed = jnp.where(even, lane, (lane + 65) & 127)
    back_order = jnp.where(mixed < 64, mixed, mixed - 63) + jnp.where(even, 0, 64)
    for pair in range(2 * NB):
        value = jnp.where(left[None], facing(2 * pair, 0), facing(2 * pair + 1, 1))
        for field in range(NF):
            unit = pair // 2 * NF + field
            if pair % 2 == 0:
                halo_j[unit] = value[field]
            else:
                halo_k[unit] = permuted(value[field], back_order)

    first = jnp.full((ROWS, 128), row, jnp.int32) == 0
    last = jnp.full((ROWS, 128), row, jnp.int32) == lines - 1
    top, bottom = level == 0, level == ROWS - 1
    k_low, k_high = (lane & 63) == 0, (lane & 63) == 63
    left_wide = lax.broadcasted_iota(jnp.int32, (PAIRS, 128), 1) < 64

    def line_copy(unit, step):
        target = lax.rem(row + step, lines)
        return pltpu.make_async_remote_copy(
            src_ref=sent.at[unit, pl.ds(target * PAIRS, PAIRS), :],
            dst_ref=lines_in.at[unit, row],
            send_sem=line_send.at[unit],
            recv_sem=line_recv.at[unit],
            device_id=(me, target),
            device_id_type=MESH,
        )

    def sweep_jk(unit, carry):
        block, field = unit // NF, lax.rem(unit, NF)

        @pl.when(field == 0)
        def _():
            for side in (0, 1):
                rim_copy(block, side).wait_recv()

        ahead, behind = [], []
        middle = jnp.float32(0.0)
        for direction in range(3):
            diffuse = viscous[direction, block, field]
            half_speed = 0.5 * advection[direction, block, field]
            ahead.append(diffuse - half_speed)
            behind.append(diffuse + half_speed)
            middle = middle - 2.0 * diffuse
        j_rows, k_rows = halo_j[unit], halo_k[unit]
        cells = [points[unit, pl.ds(pair * ROWS, ROWS), :] for pair in range(PAIRS)]
        turns = [pltpu.roll(cell, 64, axis=1) for cell in cells]
        summed = []
        for pair in range(PAIRS):
            cell, turn = cells[pair], turns[pair]
            below = jnp.broadcast_to(rim_in[0, unit, pl.ds(pair, 1), :], (ROWS, 128))
            above = jnp.broadcast_to(rim_in[1, unit, pl.ds(pair, 1), :], (ROWS, 128))
            below = jnp.where(first, cell, below)
            above = jnp.where(last, cell, above)
            i_minus = jnp.where(top, below, pltpu.roll(cell, 1, axis=0))
            i_plus = jnp.where(bottom, above, pltpu.roll(cell, ROWS - 1, axis=0))
            j_minus = jnp.where(left, turns[pair - 1] if pair else j_rows, turn)
            j_plus = jnp.where(left, turn, turns[pair + 1] if pair < PAIRS - 1 else j_rows)
            edge = pltpu.roll(k_rows, (128 - 2 * pair) % 128, axis=1) if pair else k_rows
            k_minus = jnp.where(k_low, edge, pltpu.roll(cell, 1, axis=1))
            k_plus = jnp.where(k_high, edge, pltpu.roll(cell, 127, axis=1))
            summed.append(
                middle * cell
                + (ahead[0] * i_plus + behind[0] * i_minus)
                + (ahead[1] * j_plus + behind[1] * j_minus)
                + (ahead[2] * k_plus + behind[2] * k_minus)
            )
        high, low = split(jnp.concatenate(summed, axis=0))
        inverse_k = weight_k[unit]
        both = lax.dot_general(
            jnp.concatenate([high, low], axis=1),
            jnp.concatenate([inverse_k, inverse_k], axis=1),
            (((1,), (1,)), ((), ())),
            preferred_element_type=F32,
        )
        turned[...] = both[:, :128] + both[:, 128:]
        columns = []
        for step in range(0, ROWS, 2):
            one = turned[pl.ds(step, PAIRS, stride=ROWS), :]
            two = turned[pl.ds(step + 1, PAIRS, stride=ROWS), :]
            evens = jnp.where(left_wide, one, pltpu.roll(two, 64, axis=1))
            odds = jnp.where(left_wide, pltpu.roll(one, 64, axis=1), two)
            columns.append(jnp.concatenate([evens, odds], axis=0))
        after = sweep(weight_j[unit], jnp.concatenate(columns, axis=1))
        for step in range(0, ROWS, 2):
            evens = after[:PAIRS, step * 64 : step * 64 + 128]
            odds = after[PAIRS:, step * 64 : step * 64 + 128]
            sent[unit, pl.ds(step, PAIRS, stride=ROWS), :] = jnp.where(
                left_wide, evens, pltpu.roll(odds, 64, axis=1)
            )
            sent[unit, pl.ds(step + 1, PAIRS, stride=ROWS), :] = jnp.where(
                left_wide, pltpu.roll(evens, 64, axis=1), odds
            )
        lines_in[unit, row] = sent[unit, pl.ds(row * PAIRS, PAIRS), :]
        for step in (4, 3, 5, 2, 6, 1, 7):
            line_copy(unit, step).start()
        return carry

    def sweep(weight, value):
        high, low = split(value)
        return jnp.dot(
            jnp.concatenate([weight, weight], axis=1),
            jnp.concatenate([high, high, low, low], axis=0),
            preferred_element_type=F32,
        )

    lax.fori_loop(0, NU, sweep_jk, 0)

    others = pl.ds(0, lines - 1)

    def sweep_i(unit, carry):
        pltpu.make_async_copy(
            lines_in.at[unit, others], lines_in.at[unit, others], line_recv.at[unit]
        ).wait()
        values = lines_in[unit]
        columns = [
            values[:, pair * ROWS : (pair + 1) * ROWS, :].reshape(NL, 128) for pair in range(4)
        ]
        result[unit] = sweep(weight_i[unit], jnp.concatenate(columns, axis=1))
        pltpu.make_async_copy(result.at[unit], out.at[unit], out_sem).start()
        return carry

    lax.fori_loop(0, NU, sweep_i, 0)

    def finish(unit, carry):
        pltpu.make_async_copy(
            lines_in.at[unit, others], lines_in.at[unit, others], line_send.at[unit]
        ).wait()
        return carry

    lax.fori_loop(0, NU, finish, 0)
    for block in range(NB):
        for side in (0, 1):
            rim_copy(block, side).wait_send()
    pltpu.make_async_copy(result, out, out_sem).wait()


def on_device(state, viscous, advection, sweep_inverse, face_links):
    blks, lines = lax.axis_size("blk"), lax.axis_size("line")
    blocks_here, fields, rows_here, plane = state.shape
    smem = pl.BlockSpec(memory_space=pltpu.SMEM)
    anywhere = pl.BlockSpec(memory_space=pl.ANY)
    far = pl.BlockSpec(memory_space=pltpu.HBM)
    dma = pltpu.SemaphoreType.DMA
    out = pl.pallas_call(
        functools.partial(kernel, blks, lines),
        out_shape=jax.ShapeDtypeStruct((NU, NL, plane // lines), F32),
        in_specs=[smem, smem, smem, far, far],
        out_specs=anywhere,
        scratch_shapes=[
            pltpu.VMEM((NU, PAIRS * ROWS, 128), F32),
            pltpu.VMEM((3 * NU, NL, NL), F32),
            pltpu.VMEM((NU, 256, 128), BF16),
            pltpu.VMEM((NU, NL, 128), BF16),
            pltpu.VMEM((NU, NL, 128), BF16),
            pltpu.VMEM((8, CODES), jnp.int32),
            pltpu.SMEM((8, CODES), jnp.int32),
            pltpu.VMEM((2 * FACES, NF, ROWS, 128), F32),
            pltpu.VMEM((blks, NF, ROWS, 128), F32),
            pltpu.VMEM((blks, NF, ROWS, 128), F32),
            pltpu.VMEM((2, NU, PAIRS, 128), F32),
            pltpu.VMEM((2, NU, PAIRS, 128), F32),
            pltpu.VMEM((NU, ROWS, 128), F32),
            pltpu.VMEM((NU, ROWS, 128), F32),
            pltpu.VMEM((PAIRS * ROWS, 128), F32),
            pltpu.VMEM((NU, PAIRS * ROWS, 128), F32),
            pltpu.VMEM((NU, lines, PAIRS, 128), F32),
            pltpu.VMEM((NU, NL, plane // lines), F32),
            dma, dma, dma, dma((2, NB)), dma((2, NB)), dma, dma, dma((NU,)), dma((NU,)), dma,
        ],
        compiler_params=pltpu.CompilerParams(
            collective_id=0, has_side_effects=True, vmem_limit_bytes=63 * 1024 * 1024
        ),
        name="implicit_update",
    )(
        face_links.transpose(2, 0, 1),
        viscous.transpose(1, 0, 2),
        advection.transpose(1, 0, 2),
        state.reshape(NU, rows_here, plane),
        sweep_inverse.reshape(3 * NU, NL, NL),
    )
    return out.reshape(blocks_here, fields, NL, plane // lines)


def solution(mesh):
    in_specs = (
        P("blk", None, "line", None),
        P("blk", None, None),
        P("blk", None, None),
        P("blk", None, None, None, None),
        P("blk", None, None),
    )
    out_specs = P("blk", None, None, "line")
    return jax.shard_map(
        on_device, mesh=mesh, in_specs=in_specs, out_specs=out_specs, check_vma=False
    )
```

```python
import functools

import jax
import jax.numpy as jnp
from jax import lax
from jax.experimental import pallas as pl
from jax.experimental.pallas import tpu as pltpu
from jax.sharding import PartitionSpec as P

MESH = pl.DeviceIdType.MESH
F32 = jnp.float32
BF16 = jnp.bfloat16

NB = 4
NF = 5
NU = NB * NF
NL = 64
ROWS = 8
PAIRS = 32
FACES = 4 * NB
CODES = 128
GROUPS = ((0, 1), (1, 2), (3, 2))


def link_codes(links, blocks_here, blks):
    lane = lax.broadcasted_iota(jnp.int32, (8, CODES), 1)
    target, slot = lane >> 1, lane & 1
    number = lane & (FACES - 1)
    faces = []
    for face in range(FACES):
        neighbor, their, flip = (links[part, face // 4, face % 4] for part in range(3))
        peer = jnp.where(neighbor >= 0, neighbor // blocks_here, -1)
        faces.append((peer, lax.rem(neighbor, blocks_here) * 4 + their, flip))
    sent = jnp.zeros_like(lane)
    seen = jnp.zeros_like(lane)
    peers = jnp.zeros_like(lane)
    theirs = jnp.zeros_like(lane)
    for face, (peer, their, flip) in enumerate(faces):
        match = target == peer
        sent = jnp.where(match & (seen == slot), 2 * face + flip, sent)
        seen = jnp.where(match, seen + 1, seen)
        peers = jnp.where(number == face, peer, peers)
        theirs = jnp.where(number == face, their, theirs)
    place = jnp.zeros_like(lane)
    for peer, their, _ in faces:
        place = jnp.where((peers == peer) & (theirs > their), place + 1, place)
    source = jnp.where(peers < 0, 0, peers)
    place = jnp.where(peers < 0, 2, place)
    return jnp.where(lane < 2 * blks, sent, jnp.where(lane < 2 * blks + FACES, source, place))


def permuted(value, order):
    return jnp.take_along_axis(value, order, axis=1, mode="promise_in_bounds")


def split(value):
    high = value.astype(BF16)
    low = (value - high.astype(F32)).astype(BF16)
    return high, low


def kernel(
    blks, lines,
    links, viscous, advection, state, inverse, out,
    points, inv, weight_k, weight_j, weight_i, codes_out, codes, table, slots, arrived,
    rim_out, rim_in, halo_j, halo_k, turned, sent, lines_in, result,
    load_sem, inv_sem, codes_sem, rim_send, rim_recv, face_send, face_recv, line_send, line_recv, out_sem,
):
    me = lax.axis_index("blk")
    row = lax.axis_index("line")

    def load(pair):
        return pltpu.make_async_copy(
            state.at[:, :, pl.ds(pair * 128, 128)],
            points.at[:, pl.ds(pair * ROWS, ROWS), :],
            load_sem,
        )

    for pair in range(PAIRS):
        load(pair).start()
    inv_copy = pltpu.make_async_copy(inverse, inv, inv_sem)
    inv_copy.start()

    barrier = pltpu.get_barrier_semaphore()

    def greet(target, line):
        pl.semaphore_signal(barrier, inc=1, device_id=(target, line), device_id_type=MESH)

    side = 4
    mine = (me // (2 * side), lax.rem(me // 2, side), lax.rem(me, 2))
    away = [(y, x, core) for y in range(side) for x in range(side) for core in range(2)]
    away.sort(key=lambda step: -min(step[0], side - step[0]) - min(step[1], side - step[1]))
    for step in sorted(range(1, lines), key=lambda step: -min(step, lines - step)):
        greet(me, lax.rem(row + step, lines))
    for y, x, core in away:
        if y or x or core:
            ring_y, ring_x = lax.rem(mine[0] + y, side), lax.rem(mine[1] + x, side)
            greet((ring_y * side + ring_x) * 2 + lax.rem(mine[2] + core, 2), row)

    codes_out[...] = link_codes(links, NB, blks)
    codes_copy = pltpu.make_async_copy(codes_out, codes, codes_sem)
    codes_copy.start()

    lane = lax.broadcasted_iota(jnp.int32, (ROWS, 128), 1)
    level = lax.broadcasted_iota(jnp.int32, (ROWS, 128), 0)
    left = lane < 64
    even = (lane & 1) == 0
    point = lane & 63

    pltpu.make_async_copy(points, points, load_sem).wait()

    def take_rims(block, carry):
        for field in range(NF):
            unit = block * NF + field
            rim_out[0, field, block] = points[unit, pl.ds(0, PAIRS, stride=ROWS), :]
            rim_out[1, field, block] = points[unit, pl.ds(ROWS - 1, PAIRS, stride=ROWS), :]
        return carry

    lax.fori_loop(0, NB, take_rims, 0)

    key = ((lane + 1) & 63) >> 1
    bits = [((key >> bit) & 1) == 1 for bit in range(5)]

    def mixed_low(where):
        return (where & 1) * 64 + (where & 62)

    low_order = [mixed_low(point), mixed_low(63 - point)]
    k_orders = low_order + [(order + 63) & 127 for order in low_order]
    j_orders = [point, 63 - point, 64 + point, 127 - point]

    def take_faces(block, carry):
        for field in range(NF):
            unit = block * NF + field
            cells = [points[unit, pl.ds(pair * ROWS, ROWS), :] for pair in range(PAIRS)]
            j_faces = jnp.where(left, cells[0], cells[PAIRS - 1])
            tiles = [pltpu.roll(cell, 2 * pair, axis=1) for pair, cell in enumerate(cells)]
            for bit in bits:
                tiles = [
                    jnp.where(bit, high, low) for low, high in zip(tiles[::2], tiles[1::2])
                ]
            for number, order in enumerate(j_orders):
                table[8 * block + number, field] = permuted(j_faces, order)
            for number, order in enumerate(k_orders):
                table[8 * block + 4 + number, field] = permuted(tiles[0], order)
        return carry

    lax.fori_loop(0, NB, take_faces, 0)
    codes_copy.wait()

    def fill_slots(target, carry):
        slots[target] = jnp.where(
            left[None], table[codes[0, 2 * target]], table[codes[0, 2 * target + 1]]
        )
        return carry

    lax.fori_loop(0, blks, fill_slots, 0)

    pl.semaphore_wait(barrier, blks + lines - 2)

    def rim_copy(group, side):
        fields = pl.ds(*GROUPS[group])
        return pltpu.make_async_remote_copy(
            src_ref=rim_out.at[side, fields],
            dst_ref=rim_in.at[1 - side, fields],
            send_sem=rim_send.at[side, group],
            recv_sem=rim_recv.at[1 - side, group],
            device_id=(me, lax.rem(row + (lines - 1 if side == 0 else 1), lines)),
            device_id_type=MESH,
        )

    for group, (field, fields) in enumerate(GROUPS):
        for side in (0, 1):
            rim_copy(group, side).start()

        def send_faces(step, carry):
            target = lax.rem(me + step, blks)
            pltpu.make_async_remote_copy(
                src_ref=slots.at[target, pl.ds(field, fields)],
                dst_ref=arrived[group].at[me],
                send_sem=face_send.at[group],
                recv_sem=face_recv.at[group],
                device_id=(target, row),
                device_id_type=MESH,
            ).start()
            return carry

        lax.fori_loop(1, blks, send_faces, 0)

    def all_faces(group, sems):
        part = arrived[group].at[pl.ds(0, blks - 1)]
        return pltpu.make_async_copy(part, part, sems.at[group])

    inv_copy.wait()
    deep = lax.broadcasted_iota(jnp.int32, (NL, 128), 0)
    wide = lax.broadcasted_iota(jnp.int32, (NL, 128), 1)
    ones = jnp.ones((NL, 128), F32)
    zeros = jnp.zeros((NL, 128), F32)
    at_left = jnp.where(deep == wide, ones, zeros).astype(BF16)
    at_right = jnp.where(deep + NL == wide, ones, zeros).astype(BF16)
    column = wide & 63
    order = 2 * (column & 31) + (column >> 5)
    picked = jnp.where(deep == order, ones, zeros)
    pick_left = jnp.where(wide < 64, picked, zeros).astype(BF16)
    pick_right = jnp.where(wide < 64, zeros, picked).astype(BF16)

    def place(value, where):
        return jnp.dot(value, where, preferred_element_type=F32)

    def make_weights(unit, carry):
        block, field = unit // NF, lax.rem(unit, NF)
        base = block * 3 * NF + field
        high, low = split(inv[base + 2 * NF])
        weight_k[unit, 0:64] = place(high, at_left).astype(BF16)
        weight_k[unit, 64:128] = place(high, at_right).astype(BF16)
        weight_k[unit, 128:192] = place(low, at_left).astype(BF16)
        weight_k[unit, 192:256] = place(low, at_right).astype(BF16)
        along_j = jnp.concatenate(
            [
                inv[base + NF, pl.ds(0, PAIRS, stride=2), :],
                inv[base + NF, pl.ds(1, PAIRS, stride=2), :],
            ],
            axis=0,
        )
        high, low = split(along_j)
        weight_j[unit] = (place(high, pick_left) + place(low, pick_right)).astype(BF16)
        high, low = split(inv[base])
        weight_i[unit] = (place(high, at_left) + place(low, at_right)).astype(BF16)
        return carry

    lax.fori_loop(0, NU, make_weights, 0)

    mixed = jnp.where(even, lane, (lane + 65) & 127)
    back_order = jnp.where(mixed < 64, mixed, mixed - 63) + jnp.where(even, 0, 64)

    def facing(face, half, group, field):
        source = codes[0, 2 * blks + face]
        slots_of = jnp.full((ROWS, 128), codes[0, 2 * blks + FACES + face], jnp.int32)
        value = arrived[group][source, field - GROUPS[group][0]]
        value = jnp.where(slots_of == half, value, pltpu.roll(value, 64, axis=1))
        return jnp.where(slots_of == 2, table[2 * face, field], value)

    def take_halos(group):
        for side in (0, 1):
            rim_copy(group, side).wait_recv()
        all_faces(group, face_recv).wait()
        for field in range(GROUPS[group][0], sum(GROUPS[group])):
            for pair in range(2 * NB):
                low = facing(2 * pair, 0, group, field)
                high = facing(2 * pair + 1, 1, group, field)
                value = jnp.where(left, low, high)
                unit = pair // 2 * NF + field
                if pair % 2 == 0:
                    halo_j[unit] = value
                else:
                    halo_k[unit] = permuted(value, back_order)

    first = jnp.full((ROWS, 128), row, jnp.int32) == 0
    last = jnp.full((ROWS, 128), row, jnp.int32) == lines - 1
    top, bottom = level == 0, level == ROWS - 1
    k_low, k_high = (lane & 63) == 0, (lane & 63) == 63
    left_wide = lax.broadcasted_iota(jnp.int32, (PAIRS, 128), 1) < 64

    def line_copy(unit, step):
        target = lax.rem(row + step, lines)
        return pltpu.make_async_remote_copy(
            src_ref=sent.at[unit, pl.ds(target * PAIRS, PAIRS), :],
            dst_ref=lines_in.at[unit, row],
            send_sem=line_send.at[unit],
            recv_sem=line_recv.at[unit],
            device_id=(me, target),
            device_id_type=MESH,
        )

    def unit_of(turn):
        field, block = turn // NB, lax.rem(turn, NB)
        return field, block, block * NF + field

    def sweep_jk(turn, carry):
        field, block, unit = unit_of(turn)
        for group in range(len(GROUPS)):
            pl.when(turn == NB * GROUPS[group][0])(functools.partial(take_halos, group))
        ahead, behind = [], []
        middle = jnp.float32(0.0)
        for direction in range(3):
            diffuse = viscous[direction, block, field]
            half_speed = 0.5 * advection[direction, block, field]
            ahead.append(diffuse - half_speed)
            behind.append(diffuse + half_speed)
            middle = middle - 2.0 * diffuse
        j_rows, k_rows = halo_j[unit], halo_k[unit]
        cells = [points[unit, pl.ds(pair * ROWS, ROWS), :] for pair in range(PAIRS)]
        turns = [pltpu.roll(cell, 64, axis=1) for cell in cells]
        summed = []
        for pair in range(PAIRS):
            cell, turn = cells[pair], turns[pair]
            below = jnp.broadcast_to(rim_in[0, field, block, pl.ds(pair, 1), :], (ROWS, 128))
            above = jnp.broadcast_to(rim_in[1, field, block, pl.ds(pair, 1), :], (ROWS, 128))
            below = jnp.where(first, cell, below)
            above = jnp.where(last, cell, above)
            i_minus = jnp.where(top, below, pltpu.roll(cell, 1, axis=0))
            i_plus = jnp.where(bottom, above, pltpu.roll(cell, ROWS - 1, axis=0))
            j_minus = jnp.where(left, turns[pair - 1] if pair else j_rows, turn)
            j_plus = jnp.where(left, turn, turns[pair + 1] if pair < PAIRS - 1 else j_rows)
            edge = pltpu.roll(k_rows, (128 - 2 * pair) % 128, axis=1) if pair else k_rows
            k_minus = jnp.where(k_low, edge, pltpu.roll(cell, 1, axis=1))
            k_plus = jnp.where(k_high, edge, pltpu.roll(cell, 127, axis=1))
            summed.append(
                middle * cell
                + (ahead[0] * i_plus + behind[0] * i_minus)
                + (ahead[1] * j_plus + behind[1] * j_minus)
                + (ahead[2] * k_plus + behind[2] * k_minus)
            )
        high, low = split(jnp.concatenate(summed, axis=0))
        inverse_k = weight_k[unit]
        both = lax.dot_general(
            jnp.concatenate([high, low], axis=1),
            jnp.concatenate([inverse_k, inverse_k], axis=1),
            (((1,), (1,)), ((), ())),
            preferred_element_type=F32,
        )
        turned[...] = both[:, :128] + both[:, 128:]
        columns = []
        for step in range(0, ROWS, 2):
            one = turned[pl.ds(step, PAIRS, stride=ROWS), :]
            two = turned[pl.ds(step + 1, PAIRS, stride=ROWS), :]
            evens = jnp.where(left_wide, one, pltpu.roll(two, 64, axis=1))
            odds = jnp.where(left_wide, pltpu.roll(one, 64, axis=1), two)
            columns.append(jnp.concatenate([evens, odds], axis=0))
        after = sweep(weight_j[unit], jnp.concatenate(columns, axis=1))
        for step in range(0, ROWS, 2):
            evens = after[:PAIRS, step * 64 : step * 64 + 128]
            odds = after[PAIRS:, step * 64 : step * 64 + 128]
            sent[unit, pl.ds(step, PAIRS, stride=ROWS), :] = jnp.where(
                left_wide, evens, pltpu.roll(odds, 64, axis=1)
            )
            sent[unit, pl.ds(step + 1, PAIRS, stride=ROWS), :] = jnp.where(
                left_wide, pltpu.roll(evens, 64, axis=1), odds
            )
        lines_in[unit, row] = sent[unit, pl.ds(row * PAIRS, PAIRS), :]
        for step in (4, 3, 5, 2, 6, 1, 7):
            line_copy(unit, step).start()
        return carry

    def sweep(weight, value):
        high, low = split(value)
        return jnp.dot(
            jnp.concatenate([weight, weight], axis=1),
            jnp.concatenate([high, high, low, low], axis=0),
            preferred_element_type=F32,
        )

    lax.fori_loop(0, NU, sweep_jk, 0)

    others = pl.ds(0, lines - 1)

    def sweep_i(turn, carry):
        unit = unit_of(turn)[2]
        pltpu.make_async_copy(
            lines_in.at[unit, others], lines_in.at[unit, others], line_recv.at[unit]
        ).wait()
        values = lines_in[unit]
        columns = [
            values[:, pair * ROWS : (pair + 1) * ROWS, :].reshape(NL, 128) for pair in range(4)
        ]
        result[unit] = sweep(weight_i[unit], jnp.concatenate(columns, axis=1))
        pltpu.make_async_copy(result.at[unit], out.at[unit], out_sem).start()
        return carry

    lax.fori_loop(0, NU, sweep_i, 0)

    def finish(unit, carry):
        pltpu.make_async_copy(
            lines_in.at[unit, others], lines_in.at[unit, others], line_send.at[unit]
        ).wait()
        return carry

    lax.fori_loop(0, NU, finish, 0)
    for group in range(len(GROUPS)):
        all_faces(group, face_send).wait()
        for side in (0, 1):
            rim_copy(group, side).wait_send()
    pltpu.make_async_copy(result, out, out_sem).wait()


def on_device(state, viscous, advection, sweep_inverse, face_links):
    blks, lines = lax.axis_size("blk"), lax.axis_size("line")
    blocks_here, fields, rows_here, plane = state.shape
    smem = pl.BlockSpec(memory_space=pltpu.SMEM)
    anywhere = pl.BlockSpec(memory_space=pl.ANY)
    far = pl.BlockSpec(memory_space=pltpu.HBM)
    dma = pltpu.SemaphoreType.DMA
    parts = len(GROUPS)
    out = pl.pallas_call(
        functools.partial(kernel, blks, lines),
        out_shape=pltpu.VMEM((NU, NL, plane // lines), F32),
        in_specs=[smem, smem, smem, far, far],
        out_specs=anywhere,
        scratch_shapes=[
            pltpu.VMEM((NU, PAIRS * ROWS, 128), F32),
            pltpu.VMEM((3 * NU, NL, NL), F32),
            pltpu.VMEM((NU, 256, 128), BF16),
            pltpu.VMEM((NU, NL, 128), BF16),
            pltpu.VMEM((NU, NL, 128), BF16),
            pltpu.VMEM((8, CODES), jnp.int32),
            pltpu.SMEM((8, CODES), jnp.int32),
            pltpu.VMEM((2 * FACES, NF, ROWS, 128), F32),
            pltpu.VMEM((blks, NF, ROWS, 128), F32),
            [pltpu.VMEM((blks, fields, ROWS, 128), F32) for _, fields in GROUPS],
            pltpu.VMEM((2, NF, NB, PAIRS, 128), F32),
            pltpu.VMEM((2, NF, NB, PAIRS, 128), F32),
            pltpu.VMEM((NU, ROWS, 128), F32),
            pltpu.VMEM((NU, ROWS, 128), F32),
            pltpu.VMEM((PAIRS * ROWS, 128), F32),
            pltpu.VMEM((NU, PAIRS * ROWS, 128), F32),
            pltpu.VMEM((NU, lines, PAIRS, 128), F32),
            pltpu.VMEM((NU, NL, plane // lines), F32),
            dma, dma, dma, dma((2, parts)), dma((2, parts)), dma((parts,)), dma((parts,)), dma((NU,)), dma((NU,)), dma,
        ],
        compiler_params=pltpu.CompilerParams(
            collective_id=0, has_side_effects=True, vmem_limit_bytes=60 * 1024 * 1024
        ),
        name="implicit_update",
    )(
        face_links.transpose(2, 0, 1),
        viscous.transpose(1, 0, 2),
        advection.transpose(1, 0, 2),
        state.reshape(NU, rows_here, plane),
        sweep_inverse.reshape(3 * NU, NL, NL),
    )
    return out.reshape(blocks_here, fields, NL, plane // lines)


def solution(mesh):
    in_specs = (
        P("blk", None, "line", None),
        P("blk", None, None),
        P("blk", None, None),
        P("blk", None, None, None, None),
        P("blk", None, None),
    )
    out_specs = P("blk", None, None, "line")
    return jax.shard_map(
        on_device, mesh=mesh, in_specs=in_specs, out_specs=out_specs, check_vma=False
    )
```

```python
import functools

import jax
import jax.numpy as jnp
from jax import lax
from jax.experimental import pallas as pl
from jax.experimental.pallas import tpu as pltpu
from jax.sharding import PartitionSpec as P

MESH = pl.DeviceIdType.MESH
F32 = jnp.float32
BF16 = jnp.bfloat16

NB = 4
NF = 5
NU = NB * NF
NL = 64
ROWS = 8
PAIRS = 32
FACES = 4 * NB
CODES = 128
GROUPS = ((0, 1), (1, 2), (3, 2))


def link_codes(links, blocks_here, blks):
    lane = lax.broadcasted_iota(jnp.int32, (8, CODES), 1)
    target, slot = lane >> 1, lane & 1
    number = lane & (FACES - 1)
    faces = []
    for face in range(FACES):
        neighbor, their, flip = (links[part, face // 4, face % 4] for part in range(3))
        peer = jnp.where(neighbor >= 0, neighbor // blocks_here, -1)
        faces.append((peer, lax.rem(neighbor, blocks_here) * 4 + their, flip))
    sent = jnp.zeros_like(lane)
    seen = jnp.zeros_like(lane)
    peers = jnp.zeros_like(lane)
    theirs = jnp.zeros_like(lane)
    for face, (peer, their, flip) in enumerate(faces):
        match = target == peer
        sent = jnp.where(match & (seen == slot), 2 * face + flip, sent)
        seen = jnp.where(match, seen + 1, seen)
        peers = jnp.where(number == face, peer, peers)
        theirs = jnp.where(number == face, their, theirs)
    place = jnp.zeros_like(lane)
    for peer, their, _ in faces:
        place = jnp.where((peers == peer) & (theirs > their), place + 1, place)
    source = jnp.where(peers < 0, 0, peers)
    place = jnp.where(peers < 0, 2, place)
    return jnp.where(lane < 2 * blks, sent, jnp.where(lane < 2 * blks + FACES, source, place))


def permuted(value, order):
    return jnp.take_along_axis(value, order, axis=1, mode="promise_in_bounds")


def split(value):
    high = value.astype(BF16)
    low = (value - high.astype(F32)).astype(BF16)
    return high, low


def kernel(
    blks, lines,
    links_far, viscous_far, advection_far, state, inverse, out,
    links, viscous, advection,
    points, inv, weight_k, weight_j, weight_i, codes_out, codes, table, slots, arrived,
    rim_out, rim_in, halo_j, halo_k, turned, sent, lines_in,
    small_sem, load_sem, inv_sem, codes_sem, rim_send, rim_recv, face_send, face_recv, line_send, line_recv,
):
    me = lax.axis_index("blk")
    row = lax.axis_index("line")

    def load(pair):
        return pltpu.make_async_copy(
            state.at[:, :, pl.ds(pair * 128, 128)],
            points.at[:, pl.ds(pair * ROWS, ROWS), :],
            load_sem,
        )

    barrier = pltpu.get_barrier_semaphore()

    def greet(target, line):
        pl.semaphore_signal(barrier, inc=1, device_id=(target, line), device_id_type=MESH)

    side = 4
    mine = (me // (2 * side), lax.rem(me // 2, side), lax.rem(me, 2))
    away = [(y, x, core) for y in range(side) for x in range(side) for core in range(2)]
    away.sort(key=lambda step: -min(step[0], side - step[0]) - min(step[1], side - step[1]))
    for step in sorted(range(1, lines), key=lambda step: -min(step, lines - step)):
        greet(me, lax.rem(row + step, lines))
    for y, x, core in away:
        if y or x or core:
            ring_y, ring_x = lax.rem(mine[0] + y, side), lax.rem(mine[1] + x, side)
            greet((ring_y * side + ring_x) * 2 + lax.rem(mine[2] + core, 2), row)

    small = [
        pltpu.make_async_copy(source, target, small_sem.at[number])
        for number, (source, target) in enumerate(
            ((links_far, links), (viscous_far, viscous), (advection_far, advection))
        )
    ]
    for copy in small:
        copy.start()
    for pair in range(PAIRS):
        load(pair).start()
    inv_copy = pltpu.make_async_copy(inverse, inv, inv_sem)
    inv_copy.start()

    for copy in small:
        copy.wait()
    codes_out[...] = link_codes(links, NB, blks)
    codes_copy = pltpu.make_async_copy(codes_out, codes, codes_sem)
    codes_copy.start()

    lane = lax.broadcasted_iota(jnp.int32, (ROWS, 128), 1)
    level = lax.broadcasted_iota(jnp.int32, (ROWS, 128), 0)
    left = lane < 64
    even = (lane & 1) == 0
    point = lane & 63

    pltpu.make_async_copy(points, points, load_sem).wait()

    def take_rims(block, carry):
        for field in range(NF):
            unit = block * NF + field
            rim_out[0, field, block] = points[unit, pl.ds(0, PAIRS, stride=ROWS), :]
            rim_out[1, field, block] = points[unit, pl.ds(ROWS - 1, PAIRS, stride=ROWS), :]
        return carry

    lax.fori_loop(0, NB, take_rims, 0)

    key = ((lane + 1) & 63) >> 1
    bits = [((key >> bit) & 1) == 1 for bit in range(5)]

    def mixed_low(where):
        return (where & 1) * 64 + (where & 62)

    low_order = [mixed_low(point), mixed_low(63 - point)]
    k_orders = low_order + [(order + 63) & 127 for order in low_order]
    j_orders = [point, 63 - point, 64 + point, 127 - point]

    def take_faces(block, carry):
        for field in range(NF):
            unit = block * NF + field
            cells = [points[unit, pl.ds(pair * ROWS, ROWS), :] for pair in range(PAIRS)]
            j_faces = jnp.where(left, cells[0], cells[PAIRS - 1])
            tiles = [pltpu.roll(cell, 2 * pair, axis=1) for pair, cell in enumerate(cells)]
            for bit in bits:
                tiles = [
                    jnp.where(bit, high, low) for low, high in zip(tiles[::2], tiles[1::2])
                ]
            for number, order in enumerate(j_orders):
                table[8 * block + number, field] = permuted(j_faces, order)
            for number, order in enumerate(k_orders):
                table[8 * block + 4 + number, field] = permuted(tiles[0], order)
        return carry

    lax.fori_loop(0, NB, take_faces, 0)
    codes_copy.wait()

    def fill_slots(target, carry):
        slots[target] = jnp.where(
            left[None], table[codes[0, 2 * target]], table[codes[0, 2 * target + 1]]
        )
        return carry

    lax.fori_loop(0, blks, fill_slots, 0)

    pl.semaphore_wait(barrier, blks + lines - 2)

    def rim_copy(group, side):
        fields = pl.ds(*GROUPS[group])
        return pltpu.make_async_remote_copy(
            src_ref=rim_out.at[side, fields],
            dst_ref=rim_in.at[1 - side, fields],
            send_sem=rim_send.at[side, group],
            recv_sem=rim_recv.at[1 - side, group],
            device_id=(me, lax.rem(row + (lines - 1 if side == 0 else 1), lines)),
            device_id_type=MESH,
        )

    for group, (field, fields) in enumerate(GROUPS):
        for side in (0, 1):
            rim_copy(group, side).start()

        def send_faces(step, carry):
            target = lax.rem(me + step, blks)
            pltpu.make_async_remote_copy(
                src_ref=slots.at[target, pl.ds(field, fields)],
                dst_ref=arrived[group].at[me],
                send_sem=face_send.at[group],
                recv_sem=face_recv.at[group],
                device_id=(target, row),
                device_id_type=MESH,
            ).start()
            return carry

        lax.fori_loop(1, blks, send_faces, 0)

    def all_faces(group, sems):
        part = arrived[group].at[pl.ds(0, blks - 1)]
        return pltpu.make_async_copy(part, part, sems.at[group])

    inv_copy.wait()
    deep = lax.broadcasted_iota(jnp.int32, (NL, 128), 0)
    wide = lax.broadcasted_iota(jnp.int32, (NL, 128), 1)
    ones = jnp.ones((NL, 128), F32)
    zeros = jnp.zeros((NL, 128), F32)
    at_left = jnp.where(deep == wide, ones, zeros).astype(BF16)
    at_right = jnp.where(deep + NL == wide, ones, zeros).astype(BF16)
    column = wide & 63
    order = 2 * (column & 31) + (column >> 5)
    picked = jnp.where(deep == order, ones, zeros)
    pick_left = jnp.where(wide < 64, picked, zeros).astype(BF16)
    pick_right = jnp.where(wide < 64, zeros, picked).astype(BF16)

    def place(value, where):
        return jnp.dot(value, where, preferred_element_type=F32)

    def make_weights(unit, carry):
        block, field = unit // NF, lax.rem(unit, NF)
        base = block * 3 * NF + field
        high, low = split(inv[base + 2 * NF])
        weight_k[unit, 0:64] = place(high, at_left).astype(BF16)
        weight_k[unit, 64:128] = place(high, at_right).astype(BF16)
        weight_k[unit, 128:192] = place(low, at_left).astype(BF16)
        weight_k[unit, 192:256] = place(low, at_right).astype(BF16)
        along_j = jnp.concatenate(
            [
                inv[base + NF, pl.ds(0, PAIRS, stride=2), :],
                inv[base + NF, pl.ds(1, PAIRS, stride=2), :],
            ],
            axis=0,
        )
        high, low = split(along_j)
        weight_j[unit] = (place(high, pick_left) + place(low, pick_right)).astype(BF16)
        high, low = split(inv[base])
        weight_i[unit] = (place(high, at_left) + place(low, at_right)).astype(BF16)
        return carry

    lax.fori_loop(0, NU, make_weights, 0)

    mixed = jnp.where(even, lane, (lane + 65) & 127)
    back_order = jnp.where(mixed < 64, mixed, mixed - 63) + jnp.where(even, 0, 64)

    def facing(face, half, group, field):
        source = codes[0, 2 * blks + face]
        slots_of = jnp.full((ROWS, 128), codes[0, 2 * blks + FACES + face], jnp.int32)
        value = arrived[group][source, field - GROUPS[group][0]]
        value = jnp.where(slots_of == half, value, pltpu.roll(value, 64, axis=1))
        return jnp.where(slots_of == 2, table[2 * face, field], value)

    def take_halos(group):
        for side in (0, 1):
            rim_copy(group, side).wait_recv()
        all_faces(group, face_recv).wait()
        for field in range(GROUPS[group][0], sum(GROUPS[group])):
            for pair in range(2 * NB):
                low = facing(2 * pair, 0, group, field)
                high = facing(2 * pair + 1, 1, group, field)
                value = jnp.where(left, low, high)
                unit = pair // 2 * NF + field
                if pair % 2 == 0:
                    halo_j[unit] = value
                else:
                    halo_k[unit] = permuted(value, back_order)

    first = jnp.full((ROWS, 128), row, jnp.int32) == 0
    last = jnp.full((ROWS, 128), row, jnp.int32) == lines - 1
    top, bottom = level == 0, level == ROWS - 1
    k_low, k_high = (lane & 63) == 0, (lane & 63) == 63
    left_wide = lax.broadcasted_iota(jnp.int32, (PAIRS, 128), 1) < 64

    def line_copy(unit, step):
        target = lax.rem(row + step, lines)
        return pltpu.make_async_remote_copy(
            src_ref=sent.at[unit, pl.ds(target * PAIRS, PAIRS), :],
            dst_ref=lines_in.at[unit, row],
            send_sem=line_send.at[unit],
            recv_sem=line_recv.at[unit],
            device_id=(me, target),
            device_id_type=MESH,
        )

    def unit_of(turn):
        field, block = turn // NB, lax.rem(turn, NB)
        return field, block, block * NF + field

    def sweep_jk(turn, carry):
        field, block, unit = unit_of(turn)
        for group in range(len(GROUPS)):
            pl.when(turn == NB * GROUPS[group][0])(functools.partial(take_halos, group))
        ahead, behind = [], []
        middle = jnp.float32(0.0)
        for direction in range(3):
            diffuse = viscous[direction, block, field]
            half_speed = 0.5 * advection[direction, block, field]
            ahead.append(diffuse - half_speed)
            behind.append(diffuse + half_speed)
            middle = middle - 2.0 * diffuse
        j_rows, k_rows = halo_j[unit], halo_k[unit]
        cells = [points[unit, pl.ds(pair * ROWS, ROWS), :] for pair in range(PAIRS)]
        turns = [pltpu.roll(cell, 64, axis=1) for cell in cells]
        summed = []
        for pair in range(PAIRS):
            cell, turn = cells[pair], turns[pair]
            below = jnp.broadcast_to(rim_in[0, field, block, pl.ds(pair, 1), :], (ROWS, 128))
            above = jnp.broadcast_to(rim_in[1, field, block, pl.ds(pair, 1), :], (ROWS, 128))
            below = jnp.where(first, cell, below)
            above = jnp.where(last, cell, above)
            i_minus = jnp.where(top, below, pltpu.roll(cell, 1, axis=0))
            i_plus = jnp.where(bottom, above, pltpu.roll(cell, ROWS - 1, axis=0))
            j_minus = jnp.where(left, turns[pair - 1] if pair else j_rows, turn)
            j_plus = jnp.where(left, turn, turns[pair + 1] if pair < PAIRS - 1 else j_rows)
            edge = pltpu.roll(k_rows, (128 - 2 * pair) % 128, axis=1) if pair else k_rows
            k_minus = jnp.where(k_low, edge, pltpu.roll(cell, 1, axis=1))
            k_plus = jnp.where(k_high, edge, pltpu.roll(cell, 127, axis=1))
            summed.append(
                middle * cell
                + (ahead[0] * i_plus + behind[0] * i_minus)
                + (ahead[1] * j_plus + behind[1] * j_minus)
                + (ahead[2] * k_plus + behind[2] * k_minus)
            )
        high, low = split(jnp.concatenate(summed, axis=0))
        inverse_k = weight_k[unit]
        both = lax.dot_general(
            jnp.concatenate([high, low], axis=1),
            jnp.concatenate([inverse_k, inverse_k], axis=1),
            (((1,), (1,)), ((), ())),
            preferred_element_type=F32,
        )
        turned[...] = both[:, :128] + both[:, 128:]
        columns = []
        for step in range(0, ROWS, 2):
            one = turned[pl.ds(step, PAIRS, stride=ROWS), :]
            two = turned[pl.ds(step + 1, PAIRS, stride=ROWS), :]
            evens = jnp.where(left_wide, one, pltpu.roll(two, 64, axis=1))
            odds = jnp.where(left_wide, pltpu.roll(one, 64, axis=1), two)
            columns.append(jnp.concatenate([evens, odds], axis=0))
        after = sweep(weight_j[unit], jnp.concatenate(columns, axis=1))
        for step in range(0, ROWS, 2):
            evens = after[:PAIRS, step * 64 : step * 64 + 128]
            odds = after[PAIRS:, step * 64 : step * 64 + 128]
            sent[unit, pl.ds(step, PAIRS, stride=ROWS), :] = jnp.where(
                left_wide, evens, pltpu.roll(odds, 64, axis=1)
            )
            sent[unit, pl.ds(step + 1, PAIRS, stride=ROWS), :] = jnp.where(
                left_wide, pltpu.roll(evens, 64, axis=1), odds
            )
        lines_in[unit, row] = sent[unit, pl.ds(row * PAIRS, PAIRS), :]
        for step in (4, 3, 5, 2, 6, 1, 7):
            line_copy(unit, step).start()
        return carry

    def sweep(weight, value):
        high, low = split(value)
        return jnp.dot(
            jnp.concatenate([weight, weight], axis=1),
            jnp.concatenate([high, high, low, low], axis=0),
            preferred_element_type=F32,
        )

    lax.fori_loop(0, NU, sweep_jk, 0)

    others = pl.ds(0, lines - 1)

    def sweep_i(turn, carry):
        unit = unit_of(turn)[2]
        pltpu.make_async_copy(
            lines_in.at[unit, others], lines_in.at[unit, others], line_recv.at[unit]
        ).wait()
        values = lines_in[unit]
        columns = [
            values[:, pair * ROWS : (pair + 1) * ROWS, :].reshape(NL, 128) for pair in range(4)
        ]
        out[unit] = sweep(weight_i[unit], jnp.concatenate(columns, axis=1))
        return carry

    lax.fori_loop(0, NU, sweep_i, 0)

    def finish(unit, carry):
        pltpu.make_async_copy(
            lines_in.at[unit, others], lines_in.at[unit, others], line_send.at[unit]
        ).wait()
        return carry

    lax.fori_loop(0, NU, finish, 0)
    for group in range(len(GROUPS)):
        all_faces(group, face_send).wait()
        for side in (0, 1):
            rim_copy(group, side).wait_send()


def on_device(state, viscous, advection, sweep_inverse, face_links):
    blks, lines = lax.axis_size("blk"), lax.axis_size("line")
    blocks_here, fields, rows_here, plane = state.shape
    far = pl.BlockSpec(memory_space=pltpu.HBM)
    dma = pltpu.SemaphoreType.DMA
    parts = len(GROUPS)
    out = pl.pallas_call(
        functools.partial(kernel, blks, lines),
        out_shape=pltpu.VMEM((NU, NL, plane // lines), F32),
        in_specs=[far] * 5,
        out_specs=pl.BlockSpec(memory_space=pltpu.VMEM),
        scratch_shapes=[
            pltpu.SMEM((3, NB, 4), jnp.int32),
            pltpu.SMEM((3, NB, NF), F32),
            pltpu.SMEM((3, NB, NF), F32),
            pltpu.VMEM((NU, PAIRS * ROWS, 128), F32),
            pltpu.VMEM((3 * NU, NL, NL), F32),
            pltpu.VMEM((NU, 256, 128), BF16),
            pltpu.VMEM((NU, NL, 128), BF16),
            pltpu.VMEM((NU, NL, 128), BF16),
            pltpu.VMEM((8, CODES), jnp.int32),
            pltpu.SMEM((8, CODES), jnp.int32),
            pltpu.VMEM((2 * FACES, NF, ROWS, 128), F32),
            pltpu.VMEM((blks, NF, ROWS, 128), F32),
            [pltpu.VMEM((blks, fields, ROWS, 128), F32) for _, fields in GROUPS],
            pltpu.VMEM((2, NF, NB, PAIRS, 128), F32),
            pltpu.VMEM((2, NF, NB, PAIRS, 128), F32),
            pltpu.VMEM((NU, ROWS, 128), F32),
            pltpu.VMEM((NU, ROWS, 128), F32),
            pltpu.VMEM((PAIRS * ROWS, 128), F32),
            pltpu.VMEM((NU, PAIRS * ROWS, 128), F32),
            pltpu.VMEM((NU, lines, PAIRS, 128), F32),
            dma((3,)), dma, dma, dma, dma((2, parts)), dma((2, parts)), dma((parts,)), dma((parts,)), dma((NU,)), dma((NU,)),
        ],
        compiler_params=pltpu.CompilerParams(
            collective_id=0, has_side_effects=True, vmem_limit_bytes=60 * 1024 * 1024
        ),
        name="implicit_update",
    )(
        face_links.transpose(2, 0, 1),
        viscous.transpose(1, 0, 2),
        advection.transpose(1, 0, 2),
        state.reshape(NU, rows_here, plane),
        sweep_inverse.reshape(3 * NU, NL, NL),
    )
    return out.reshape(blocks_here, fields, NL, plane // lines)


def solution(mesh):
    in_specs = (
        P("blk", None, "line", None),
        P("blk", None, None),
        P("blk", None, None),
        P("blk", None, None, None, None),
        P("blk", None, None),
    )
    out_specs = P("blk", None, None, "line")
    return jax.shard_map(
        on_device, mesh=mesh, in_specs=in_specs, out_specs=out_specs, check_vma=False
    )
```

```python
import functools

import jax
import jax.numpy as jnp
from jax import lax
from jax.experimental import pallas as pl
from jax.experimental.pallas import tpu as pltpu
from jax.sharding import PartitionSpec as P

MESH = pl.DeviceIdType.MESH
F32 = jnp.float32
BF16 = jnp.bfloat16

NB = 4
NF = 5
NU = NB * NF
NL = 64
ROWS = 8
PAIRS = 32
FACES = 4 * NB
CODES = 128
GROUPS = ((0, 1), (1, 2), (3, 2))


def link_codes(links, blocks_here, blks):
    lane = lax.broadcasted_iota(jnp.int32, (8, CODES), 1)
    target, slot = lane >> 1, lane & 1
    number = lane & (FACES - 1)
    faces = []
    for face in range(FACES):
        neighbor, their, flip = (links[part, face // 4, face % 4] for part in range(3))
        peer = jnp.where(neighbor >= 0, neighbor // blocks_here, -1)
        faces.append((peer, lax.rem(neighbor, blocks_here) * 4 + their, flip))
    sent = jnp.zeros_like(lane)
    seen = jnp.zeros_like(lane)
    peers = jnp.zeros_like(lane)
    theirs = jnp.zeros_like(lane)
    for face, (peer, their, flip) in enumerate(faces):
        match = target == peer
        sent = jnp.where(match & (seen == slot), 2 * face + flip, sent)
        seen = jnp.where(match, seen + 1, seen)
        peers = jnp.where(number == face, peer, peers)
        theirs = jnp.where(number == face, their, theirs)
    place = jnp.zeros_like(lane)
    for peer, their, _ in faces:
        place = jnp.where((peers == peer) & (theirs > their), place + 1, place)
    source = jnp.where(peers < 0, 0, peers)
    place = jnp.where(peers < 0, 2, place)
    return jnp.where(lane < 2 * blks, sent, jnp.where(lane < 2 * blks + FACES, source, place))


def permuted(value, order):
    return jnp.take_along_axis(value, order, axis=1, mode="promise_in_bounds")


def split(value):
    high = value.astype(BF16)
    low = (value - high.astype(F32)).astype(BF16)
    return high, low


def kernel(
    blks, lines,
    links_far, viscous_far, advection_far, state, inverse, out,
    links, viscous, advection,
    points, inv, weight_k, weight_j, weight_i, codes_out, codes, table, slots, arrived,
    rim_out, rim_in, halo_j, halo_k, turned, sent, lines_in,
    small_sem, load_sem, inv_sem, codes_sem, rim_send, rim_recv, face_send, face_recv, line_send, line_recv,
):
    me = lax.axis_index("blk")
    row = lax.axis_index("line")

    def load(pair):
        return pltpu.make_async_copy(
            state.at[:, :, pl.ds(pair * 128, 128)],
            points.at[:, pl.ds(pair * ROWS, ROWS), :],
            load_sem,
        )

    barrier = pltpu.get_barrier_semaphore()

    def greet(target, line):
        pl.semaphore_signal(barrier, inc=1, device_id=(target, line), device_id_type=MESH)

    side = 4
    mine = (me // (2 * side), lax.rem(me // 2, side), lax.rem(me, 2))
    away = [(y, x, core) for y in range(side) for x in range(side) for core in range(2)]
    away.sort(key=lambda step: -min(step[0], side - step[0]) - min(step[1], side - step[1]))
    for step in sorted(range(1, lines), key=lambda step: -min(step, lines - step)):
        greet(me, lax.rem(row + step, lines))
    for y, x, core in away:
        if y or x or core:
            ring_y, ring_x = lax.rem(mine[0] + y, side), lax.rem(mine[1] + x, side)
            greet((ring_y * side + ring_x) * 2 + lax.rem(mine[2] + core, 2), row)

    small = [
        pltpu.make_async_copy(source, target, small_sem.at[number])
        for number, (source, target) in enumerate(
            ((links_far, links), (viscous_far, viscous), (advection_far, advection))
        )
    ]
    for copy in small:
        copy.start()
    for pair in range(PAIRS):
        load(pair).start()
    inv_copy = pltpu.make_async_copy(inverse, inv, inv_sem)
    inv_copy.start()

    for copy in small:
        copy.wait()
    codes_out[...] = link_codes(links, NB, blks)
    codes_copy = pltpu.make_async_copy(codes_out, codes, codes_sem)
    codes_copy.start()

    lane = lax.broadcasted_iota(jnp.int32, (ROWS, 128), 1)
    level = lax.broadcasted_iota(jnp.int32, (ROWS, 128), 0)
    left = lane < 64
    even = (lane & 1) == 0
    point = lane & 63

    pltpu.make_async_copy(points, points, load_sem).wait()

    def take_rims(block, carry):
        for field in range(NF):
            unit = block * NF + field
            rim_out[0, field, block] = points[unit, pl.ds(0, PAIRS, stride=ROWS), :]
            rim_out[1, field, block] = points[unit, pl.ds(ROWS - 1, PAIRS, stride=ROWS), :]
        return carry

    lax.fori_loop(0, NB, take_rims, 0)

    key = ((lane + 1) & 63) >> 1
    bits = [((key >> bit) & 1) == 1 for bit in range(5)]

    def mixed_low(where):
        return (where & 1) * 64 + (where & 62)

    low_order = [mixed_low(point), mixed_low(63 - point)]
    k_orders = low_order + [(order + 63) & 127 for order in low_order]
    j_orders = [point, 63 - point, 64 + point, 127 - point]

    def take_faces(block, carry):
        for field in range(NF):
            unit = block * NF + field
            cells = [points[unit, pl.ds(pair * ROWS, ROWS), :] for pair in range(PAIRS)]
            j_faces = jnp.where(left, cells[0], cells[PAIRS - 1])
            tiles = [pltpu.roll(cell, 2 * pair, axis=1) for pair, cell in enumerate(cells)]
            for bit in bits:
                tiles = [
                    jnp.where(bit, high, low) for low, high in zip(tiles[::2], tiles[1::2])
                ]
            for number, order in enumerate(j_orders):
                table[8 * block + number, field] = permuted(j_faces, order)
            for number, order in enumerate(k_orders):
                table[8 * block + 4 + number, field] = permuted(tiles[0], order)
        return carry

    lax.fori_loop(0, NB, take_faces, 0)
    codes_copy.wait()

    def fill_slots(target, carry):
        slots[target] = jnp.where(
            left[None], table[codes[0, 2 * target]], table[codes[0, 2 * target + 1]]
        )
        return carry

    lax.fori_loop(0, blks, fill_slots, 0)

    pl.semaphore_wait(barrier, blks + lines - 2)

    inner = (row > 0, row < lines - 1)

    def rim_copy(group, side):
        fields = pl.ds(*GROUPS[group])
        return pltpu.make_async_remote_copy(
            src_ref=rim_out.at[side, fields],
            dst_ref=rim_in.at[1 - side, fields],
            send_sem=rim_send.at[side, group],
            recv_sem=rim_recv.at[1 - side, group],
            device_id=(me, lax.rem(row + (lines - 1 if side == 0 else 1), lines)),
            device_id_type=MESH,
        )

    for group, (field, fields) in enumerate(GROUPS):
        for side in (0, 1):
            pl.when(inner[side])(rim_copy(group, side).start)

        def send_faces(step, carry):
            target = lax.rem(me + step, blks)
            pltpu.make_async_remote_copy(
                src_ref=slots.at[target, pl.ds(field, fields)],
                dst_ref=arrived[group].at[me],
                send_sem=face_send.at[group],
                recv_sem=face_recv.at[group],
                device_id=(target, row),
                device_id_type=MESH,
            ).start()
            return carry

        lax.fori_loop(1, blks, send_faces, 0)

    def all_faces(group, sems):
        part = arrived[group].at[pl.ds(0, blks - 1)]
        return pltpu.make_async_copy(part, part, sems.at[group])

    inv_copy.wait()
    deep = lax.broadcasted_iota(jnp.int32, (NL, 128), 0)
    wide = lax.broadcasted_iota(jnp.int32, (NL, 128), 1)
    ones = jnp.ones((NL, 128), F32)
    zeros = jnp.zeros((NL, 128), F32)
    at_left = jnp.where(deep == wide, ones, zeros).astype(BF16)
    at_right = jnp.where(deep + NL == wide, ones, zeros).astype(BF16)
    column = wide & 63
    order = 2 * (column & 31) + (column >> 5)
    picked = jnp.where(deep == order, ones, zeros)
    pick_left = jnp.where(wide < 64, picked, zeros).astype(BF16)
    pick_right = jnp.where(wide < 64, zeros, picked).astype(BF16)

    def place(value, where):
        return jnp.dot(value, where, preferred_element_type=F32)

    def make_weights(unit, carry):
        block, field = unit // NF, lax.rem(unit, NF)
        base = block * 3 * NF + field
        high, low = split(inv[base + 2 * NF])
        weight_k[unit, 0:64] = place(high, at_left).astype(BF16)
        weight_k[unit, 64:128] = place(high, at_right).astype(BF16)
        weight_k[unit, 128:192] = place(low, at_left).astype(BF16)
        weight_k[unit, 192:256] = place(low, at_right).astype(BF16)
        along_j = jnp.concatenate(
            [
                inv[base + NF, pl.ds(0, PAIRS, stride=2), :],
                inv[base + NF, pl.ds(1, PAIRS, stride=2), :],
            ],
            axis=0,
        )
        high, low = split(along_j)
        weight_j[unit] = (place(high, pick_left) + place(low, pick_right)).astype(BF16)
        high, low = split(inv[base])
        weight_i[unit] = (place(high, at_left) + place(low, at_right)).astype(BF16)
        return carry

    lax.fori_loop(0, NU, make_weights, 0)

    mixed = jnp.where(even, lane, (lane + 65) & 127)
    back_order = jnp.where(mixed < 64, mixed, mixed - 63) + jnp.where(even, 0, 64)

    def facing(face, half, group, field):
        source = codes[0, 2 * blks + face]
        slots_of = jnp.full((ROWS, 128), codes[0, 2 * blks + FACES + face], jnp.int32)
        value = arrived[group][source, field - GROUPS[group][0]]
        value = jnp.where(slots_of == half, value, pltpu.roll(value, 64, axis=1))
        return jnp.where(slots_of == 2, table[2 * face, field], value)

    def take_halos(group):
        for side in (0, 1):
            pl.when(inner[1 - side])(rim_copy(group, side).wait_recv)
        all_faces(group, face_recv).wait()
        for field in range(GROUPS[group][0], sum(GROUPS[group])):
            for pair in range(2 * NB):
                low = facing(2 * pair, 0, group, field)
                high = facing(2 * pair + 1, 1, group, field)
                value = jnp.where(left, low, high)
                unit = pair // 2 * NF + field
                if pair % 2 == 0:
                    halo_j[unit] = value
                else:
                    halo_k[unit] = permuted(value, back_order)

    first = jnp.full((ROWS, 128), row, jnp.int32) == 0
    last = jnp.full((ROWS, 128), row, jnp.int32) == lines - 1
    top, bottom = level == 0, level == ROWS - 1
    k_low, k_high = (lane & 63) == 0, (lane & 63) == 63
    left_wide = lax.broadcasted_iota(jnp.int32, (PAIRS, 128), 1) < 64

    def line_copy(unit, step):
        target = lax.rem(row + step, lines)
        return pltpu.make_async_remote_copy(
            src_ref=sent.at[unit, pl.ds(target * PAIRS, PAIRS), :],
            dst_ref=lines_in.at[unit, row],
            send_sem=line_send.at[unit],
            recv_sem=line_recv.at[unit],
            device_id=(me, target),
            device_id_type=MESH,
        )

    def unit_of(turn):
        field, block = turn // NB, lax.rem(turn, NB)
        return field, block, block * NF + field

    def sweep_jk(turn, carry):
        field, block, unit = unit_of(turn)
        for group in range(len(GROUPS)):
            pl.when(turn == NB * GROUPS[group][0])(functools.partial(take_halos, group))
        ahead, behind = [], []
        middle = jnp.float32(0.0)
        for direction in range(3):
            diffuse = viscous[direction, block, field]
            half_speed = 0.5 * advection[direction, block, field]
            ahead.append(diffuse - half_speed)
            behind.append(diffuse + half_speed)
            middle = middle - 2.0 * diffuse
        j_rows, k_rows = halo_j[unit], halo_k[unit]
        cells = [points[unit, pl.ds(pair * ROWS, ROWS), :] for pair in range(PAIRS)]
        turns = [pltpu.roll(cell, 64, axis=1) for cell in cells]
        summed = []
        for pair in range(PAIRS):
            cell, turn = cells[pair], turns[pair]
            below = jnp.broadcast_to(rim_in[0, field, block, pl.ds(pair, 1), :], (ROWS, 128))
            above = jnp.broadcast_to(rim_in[1, field, block, pl.ds(pair, 1), :], (ROWS, 128))
            below = jnp.where(first, cell, below)
            above = jnp.where(last, cell, above)
            i_minus = jnp.where(top, below, pltpu.roll(cell, 1, axis=0))
            i_plus = jnp.where(bottom, above, pltpu.roll(cell, ROWS - 1, axis=0))
            j_minus = jnp.where(left, turns[pair - 1] if pair else j_rows, turn)
            j_plus = jnp.where(left, turn, turns[pair + 1] if pair < PAIRS - 1 else j_rows)
            edge = pltpu.roll(k_rows, (128 - 2 * pair) % 128, axis=1) if pair else k_rows
            k_minus = jnp.where(k_low, edge, pltpu.roll(cell, 1, axis=1))
            k_plus = jnp.where(k_high, edge, pltpu.roll(cell, 127, axis=1))
            summed.append(
                middle * cell
                + (ahead[0] * i_plus + behind[0] * i_minus)
                + (ahead[1] * j_plus + behind[1] * j_minus)
                + (ahead[2] * k_plus + behind[2] * k_minus)
            )
        high, low = split(jnp.concatenate(summed, axis=0))
        inverse_k = weight_k[unit]
        both = lax.dot_general(
            jnp.concatenate([high, low], axis=1),
            jnp.concatenate([inverse_k, inverse_k], axis=1),
            (((1,), (1,)), ((), ())),
            preferred_element_type=F32,
        )
        turned[...] = both[:, :128] + both[:, 128:]
        columns = []
        for step in range(0, ROWS, 2):
            one = turned[pl.ds(step, PAIRS, stride=ROWS), :]
            two = turned[pl.ds(step + 1, PAIRS, stride=ROWS), :]
            evens = jnp.where(left_wide, one, pltpu.roll(two, 64, axis=1))
            odds = jnp.where(left_wide, pltpu.roll(one, 64, axis=1), two)
            columns.append(jnp.concatenate([evens, odds], axis=0))
        after = sweep(weight_j[unit], jnp.concatenate(columns, axis=1))
        for step in range(0, ROWS, 2):
            evens = after[:PAIRS, step * 64 : step * 64 + 128]
            odds = after[PAIRS:, step * 64 : step * 64 + 128]
            sent[unit, pl.ds(step, PAIRS, stride=ROWS), :] = jnp.where(
                left_wide, evens, pltpu.roll(odds, 64, axis=1)
            )
            sent[unit, pl.ds(step + 1, PAIRS, stride=ROWS), :] = jnp.where(
                left_wide, pltpu.roll(evens, 64, axis=1), odds
            )
        lines_in[unit, row] = sent[unit, pl.ds(row * PAIRS, PAIRS), :]
        for step in (4, 3, 5, 2, 6, 1, 7):
            line_copy(unit, step).start()
        return carry

    def sweep(weight, value):
        high, low = split(value)
        return jnp.dot(
            jnp.concatenate([weight, weight], axis=1),
            jnp.concatenate([high, high, low, low], axis=0),
            preferred_element_type=F32,
        )

    lax.fori_loop(0, NU, sweep_jk, 0)

    others = pl.ds(0, lines - 1)

    def sweep_i(turn, carry):
        unit = unit_of(turn)[2]
        pltpu.make_async_copy(
            lines_in.at[unit, others], lines_in.at[unit, others], line_recv.at[unit]
        ).wait()
        values = lines_in[unit]
        columns = [
            values[:, pair * ROWS : (pair + 1) * ROWS, :].reshape(NL, 128) for pair in range(4)
        ]
        out[unit] = sweep(weight_i[unit], jnp.concatenate(columns, axis=1))
        return carry

    lax.fori_loop(0, NU, sweep_i, 0)

    def finish(unit, carry):
        pltpu.make_async_copy(
            lines_in.at[unit, others], lines_in.at[unit, others], line_send.at[unit]
        ).wait()
        return carry

    lax.fori_loop(0, NU, finish, 0)
    for group in range(len(GROUPS)):
        all_faces(group, face_send).wait()
        for side in (0, 1):
            pl.when(inner[side])(rim_copy(group, side).wait_send)


def on_device(state, viscous, advection, sweep_inverse, face_links):
    blks, lines = lax.axis_size("blk"), lax.axis_size("line")
    blocks_here, fields, rows_here, plane = state.shape
    far = pl.BlockSpec(memory_space=pltpu.HBM)
    dma = pltpu.SemaphoreType.DMA
    parts = len(GROUPS)
    out = pl.pallas_call(
        functools.partial(kernel, blks, lines),
        out_shape=pltpu.VMEM((NU, NL, plane // lines), F32),
        in_specs=[far] * 5,
        out_specs=pl.BlockSpec(memory_space=pltpu.VMEM),
        scratch_shapes=[
            pltpu.SMEM((3, NB, 4), jnp.int32),
            pltpu.SMEM((3, NB, NF), F32),
            pltpu.SMEM((3, NB, NF), F32),
            pltpu.VMEM((NU, PAIRS * ROWS, 128), F32),
            pltpu.VMEM((3 * NU, NL, NL), F32),
            pltpu.VMEM((NU, 256, 128), BF16),
            pltpu.VMEM((NU, NL, 128), BF16),
            pltpu.VMEM((NU, NL, 128), BF16),
            pltpu.VMEM((8, CODES), jnp.int32),
            pltpu.SMEM((8, CODES), jnp.int32),
            pltpu.VMEM((2 * FACES, NF, ROWS, 128), F32),
            pltpu.VMEM((blks, NF, ROWS, 128), F32),
            [pltpu.VMEM((blks, fields, ROWS, 128), F32) for _, fields in GROUPS],
            pltpu.VMEM((2, NF, NB, PAIRS, 128), F32),
            pltpu.VMEM((2, NF, NB, PAIRS, 128), F32),
            pltpu.VMEM((NU, ROWS, 128), F32),
            pltpu.VMEM((NU, ROWS, 128), F32),
            pltpu.VMEM((PAIRS * ROWS, 128), F32),
            pltpu.VMEM((NU, PAIRS * ROWS, 128), F32),
            pltpu.VMEM((NU, lines, PAIRS, 128), F32),
            dma((3,)), dma, dma, dma, dma((2, parts)), dma((2, parts)), dma((parts,)), dma((parts,)), dma((NU,)), dma((NU,)),
        ],
        compiler_params=pltpu.CompilerParams(
            collective_id=0, has_side_effects=True, vmem_limit_bytes=60 * 1024 * 1024
        ),
        name="implicit_update",
    )(
        face_links.transpose(2, 0, 1),
        viscous.transpose(1, 0, 2),
        advection.transpose(1, 0, 2),
        state.reshape(NU, rows_here, plane),
        sweep_inverse.reshape(3 * NU, NL, NL),
    )
    return out.reshape(blocks_here, fields, NL, plane // lines)


def solution(mesh):
    in_specs = (
        P("blk", None, "line", None),
        P("blk", None, None),
        P("blk", None, None),
        P("blk", None, None, None, None),
        P("blk", None, None),
    )
    out_specs = P("blk", None, None, "line")
    return jax.shard_map(
        on_device, mesh=mesh, in_specs=in_specs, out_specs=out_specs, check_vma=False
    )
```
